512 devices in a mesh: ta: 8 (over z_hi, x), gx: 16 (over y, core), gy: 4 (over z_lo).
Axes of the slice: x: 4, y: 8, z: 8 (z_hi: 2, z_lo: 4; z = z_hi * 4 + z_lo), core: 2. Of those that a mesh axis runs over, the one named last changes fastest.
Arguments:
- frames: bfloat16 [8, 32, 256, 512], P('ta', None, 'gx', 'gy'), may hold values from -6 to 6
- trailing: bfloat16 [32, 256, 512], P(None, 'gx', 'gy'), may hold values from -6 to 6
Outputs:
- velocity: float32 [8, 3, 32, 256, 512], P('ta', None, None, 'gx', 'gy')
The draws below stay inside these ranges and needn't reach their ends.
All inputs are finite; a program needn't handle non-finite values.
Results may differ from the reference program's by a relative error of at most 0.0003.
Values may be sent and summed in bfloat16 or wider, within the bound.
No kernel may reach another device: no remote copies, remote signals or barrier semaphores. Data moves between devices by JAX's collectives and lax.ppermute only.
A program may use at most 64 MiB of HBM per device.

```python
import jax
import jax.numpy as jnp
from jax import lax

NZ = 32
ITERS = 3
FRAMES = 8
NX = 256
NY = 512


def block_scale(own_key, shape, cuts, least, largest):
    loudness = 1.0
    for axis_at, parts in cuts:
        steps = jax.random.uniform(jax.random.fold_in(jax.random.fold_in(own_key, 6), axis_at), (parts,), jnp.float32, least / len(cuts), largest / len(cuts))
        loudness = loudness * jnp.repeat(jnp.exp(steps), shape[axis_at] // parts).reshape((-1,) + (1,) * (len(shape) - 1 - axis_at))
    return loudness


def centred(rng, shape, width, bound, cuts=(), held_as=jnp.bfloat16):
    loudness = block_scale(rng, shape, cuts, -0.22, 0.18) if cuts else 1.0
    entries = jax.random.normal(rng, shape, jnp.float32) * width * loudness
    return jnp.minimum(jnp.maximum(entries, -bound), bound).astype(held_as)


def setup_inputs(seed: int = 0) -> dict:
    streams_of = jax.random.split(jax.random.key(seed), 3)
    return {
        "frames": centred(streams_of[0], (FRAMES, NZ, NX, NY), 1.0, 6.0, ((0, 8), (2, 16), (3, 4))),
        "trailing": centred(streams_of[1], (NZ, NX, NY), 1.0, 6.0, ((1, 16), (2, 4))),
    }


gauss_taps = (0.0625, 0.25, 0.375, 0.25, 0.0625)
smoothness = 0.01


def smooth(volume):
    result = volume
    for along in range(3):
        pad_widths = [(0, 0), (0, 0), (0, 0)]
        pad_widths[along] = (2, 2)
        padded = jnp.pad(result, pad_widths)
        extent = result.shape[along]
        summed = jnp.zeros_like(result)
        for tap_index in range(5):
            summed = summed + gauss_taps[tap_index] * lax.slice_in_dim(padded, tap_index, tap_index + extent, axis=along)
        result = summed
    return result


def gradients(first_frame, second_frame):
    summed = first_frame + second_frame
    padded = jnp.pad(summed, 1)
    slope_z = 0.25 * (padded[2:, 1:-1, 1:-1] - padded[:-2, 1:-1, 1:-1])
    slope_x = 0.25 * (padded[1:-1, 2:, 1:-1] - padded[1:-1, :-2, 1:-1])
    slope_y = 0.25 * (padded[1:-1, 1:-1, 2:] - padded[1:-1, 1:-1, :-2])
    return jnp.stack([slope_x, slope_y, slope_z]), second_frame - first_frame


def neighbour_mean(velocity):
    padded = jnp.pad(velocity, ((0, 0), (1, 1), (1, 1), (1, 1)))
    summed = padded[:, 1:-1, 2:, 1:-1] + padded[:, 1:-1, :-2, 1:-1]
    summed = summed + padded[:, 1:-1, 1:-1, 2:] + padded[:, 1:-1, 1:-1, :-2]
    summed = summed + padded[:, 2:, 1:-1, 1:-1] + padded[:, :-2, 1:-1, 1:-1]
    return summed / 6.0


def pair_flow(frame_pair):
    first_frame = smooth(frame_pair[0].astype(jnp.float32))
    second_frame = smooth(frame_pair[1].astype(jnp.float32))
    gradient, change = gradients(first_frame, second_frame)
    denominator = smoothness + jnp.sum(gradient * gradient, axis=0)
    velocity = jnp.zeros((3,) + first_frame.shape, jnp.float32)
    for iteration in range(ITERS):
        mean_flow = neighbour_mean(velocity)
        residual_term = (jnp.sum(gradient * mean_flow, axis=0) + change) / denominator
        velocity = mean_flow - gradient * residual_term[None]
    return velocity


def reference(frames, trailing):
    following = jnp.concatenate([frames[1:], trailing[None]], axis=0)
    return lax.map(pair_flow, (frames, following))
```

```python
import jax
import jax.numpy as jnp
from jax import lax
from jax.experimental import pallas as pl
from jax.experimental.pallas import tpu as pltpu
from jax.sharding import PartitionSpec as P

NZ = 32
WX = 16
LANES = 128
EDGE = 8
F32, BF16 = jnp.float32, jnp.bfloat16


def iota(shape, dim):
    return lax.broadcasted_iota(jnp.int32, shape, dim)


def group_rows(group, own, nxt, low, high):
    frame, block = divmod(group, 8)
    zs = pl.ds(4 * block, 4)
    centre = (own, nxt)[frame][zs].astype(F32)
    before, after = low[frame, zs].astype(F32), high[frame, zs].astype(F32)
    return jnp.concatenate([before, centre, after], axis=1).reshape(128, LANES)


def pack_kernel(own, nxt, low, high, to_right, to_left):
    row, lane = iota((LANES, 256), 0), iota((LANES, 256), 1)
    right = jnp.where(row >= LANES - EDGE, lane - row + LANES - EDGE, -1)
    right = jnp.where(lane < 128, right, -1)
    left = jnp.where(row < EDGE, lane - 128 - row, -1)
    left = jnp.where(lane < 128, -1, left)
    place = jnp.maximum(right, left)
    packed = jnp.zeros((128, 256), F32)
    for group in range(16):
        rows = group_rows(group, own, nxt, low, high).astype(BF16)
        pick = jnp.where(place == 8 * group, 1.0, 0.0).astype(BF16)
        packed = packed + jnp.dot(rows, pick, preferred_element_type=F32)
    to_right[...] = packed[:, :128].astype(BF16)
    to_left[...] = packed[:, 128:].astype(BF16)


def y_taps(distance):
    d = jnp.minimum(distance & 255, (-distance) & 255)
    tap = jnp.where(d == 0, 6.0, jnp.where(d == 1, 4.0, jnp.where(d == 2, 1.0, 0.0)))
    return tap * (1.0 / 4096.0)


def z_next(v, row):
    return jnp.where(row == NZ - 1, 0.0, pltpu.roll(v, NZ - 1, 0))


def z_prev(v, row):
    return jnp.where(row == 0, 0.0, pltpu.roll(v, 1, 0))


def y_next(v, other, lane):
    return pltpu.roll(jnp.where(lane == 0, other, v), LANES - 1, 1)


def y_prev(v, other, lane):
    return pltpu.roll(jnp.where(lane == LANES - 1, other, v), 1, 1)


def flow_kernel(own, nxt, low, high, from_left, from_right, out, p_ref, q_ref, s_ref, c_ref, h_ref, u_ref, v_ref):
    gx, gy = lax.axis_index("gx"), lax.axis_index("gy")
    n_gx, n_gy = lax.axis_size("gx"), lax.axis_size("gy")
    row, lane = iota((NZ, LANES), 0), iota((NZ, LANES), 1)

    main_taps = y_taps(iota((LANES, 256), 1) - iota((LANES, 256), 0)).astype(BF16)
    column = iota((EDGE, 256), 1)
    left_taps = y_taps(column - (iota((EDGE, 256), 0) + 248))
    right_taps = y_taps(column - (iota((EDGE, 256), 0) + 128))
    edges = jnp.concatenate([from_left[...], from_right[...]], axis=1)

    def smooth_y(group):
        rows = group_rows(group, own, nxt, low, high).astype(BF16)
        parts = []
        for taps in (left_taps, right_taps):
            if group > 0:
                parts.append(jnp.zeros((8 * group, 256), F32))
            parts.append(taps)
            if group < 15:
                parts.append(jnp.zeros((120 - 8 * group, 256), F32))
        edge_taps = jnp.concatenate(parts, axis=0).astype(BF16)
        return jnp.dot(rows, main_taps, preferred_element_type=F32) + jnp.dot(
            edges, edge_taps, preferred_element_type=F32
        )

    for block in range(8):
        first, second = smooth_y(block), smooth_y(8 + block)
        total, change = (first + second) * 0.25, second - first
        for i in range(4):
            z = 4 * block + i
            for tile in range(2):
                part = (slice(32 * i, 32 * i + 32), slice(128 * tile, 128 * tile + 128))
                p_ref[tile, pl.ds(z, 32, stride=NZ), :] = total[part]
                q_ref[tile, pl.ds(z, 32, stride=NZ), :] = change[part]

    def smooth_z(v):
        near = z_next(v, row) + z_prev(v, row)
        far = jnp.where(row >= NZ - 2, 0.0, pltpu.roll(v, NZ - 2, 0)) + jnp.where(
            row < 2, 0.0, pltpu.roll(v, 2, 0)
        )
        return 6.0 * v + 4.0 * near + far

    def plane_z(k, _):
        at = pl.ds(pl.multiple_of(k * NZ, NZ), NZ)
        for ref in (p_ref, q_ref):
            for tile in range(2):
                ref[tile, at, :] = smooth_z(ref[tile, at, :])
        return 0

    lax.fori_loop(3, 29, plane_z, 0)

    inside_y = jnp.where(
        lane < 64, jnp.where(gy == n_gy - 1, 0.0, 1.0), jnp.where(gy == 0, 0.0, 1.0)
    )

    def inside_x(x):
        low_out = (x < 0) & (gx == 0)
        high_out = (x >= WX) & (gx == n_gx - 1)
        return jnp.where(low_out | high_out, 0.0, 1.0)

    def plane_x(k, _):
        weight = inside_x(k - 3)
        for source, ref in ((p_ref, s_ref), (q_ref, c_ref)):
            for tile in range(2):
                planes = [
                    source[tile, pl.ds(pl.multiple_of((k + 3 + j) * NZ, NZ), NZ), :] for j in range(5)
                ]
                v = 6.0 * planes[2] + 4.0 * (planes[1] + planes[3]) + (planes[0] + planes[4])
                ref[tile, k] = v * (weight * inside_y if tile else weight)
        return 0

    lax.fori_loop(0, 22, plane_x, 0)

    def plane_h(k, _):
        for tile in range(2):
            v, other = s_ref[tile, k + 1], s_ref[1 - tile, k + 1]
            grad_x = s_ref[tile, k + 2] - s_ref[tile, k]
            grad_y = y_next(v, other, lane) - y_prev(v, other, lane)
            grad_z = z_next(v, row) - z_prev(v, row)
            denom = 0.01 + grad_x * grad_x + grad_y * grad_y + grad_z * grad_z
            scale = lax.rsqrt(denom)
            scale = scale * (1.5 - 0.5 * denom * scale * scale)
            change = c_ref[tile, k + 1] * scale
            h_ref[3, tile, k] = change
            for c, grad in enumerate((grad_x, grad_y, grad_z)):
                h = grad * scale
                h_ref[c, tile, k] = h
                u_ref[c, tile, k] = -h * change
        return 0

    lax.fori_loop(0, 20, plane_h, 0)

    def step(ref, k, k_h, tile):
        means, common = [], h_ref[3, tile, k_h]
        for c in range(3):
            v, other = ref[c, tile, k], ref[c, 1 - tile, k]
            total = ref[c, tile, k - 1] + ref[c, tile, k + 1]
            total = total + (y_next(v, other, lane) + y_prev(v, other, lane))
            total = total + (z_next(v, row) + z_prev(v, row))
            means.append(total * (1.0 / 6.0))
            common = common + h_ref[c, tile, k_h] * means[c]
        return [mean - h_ref[c, tile, k_h] * common for c, mean in enumerate(means)]

    def plane_v(k, _):
        weight = inside_x(k - 1)
        for tile in range(2):
            for c, value in enumerate(step(u_ref, k + 1, k + 1, tile)):
                v_ref[c, tile, k] = value * (weight * inside_y if tile else weight)
        return 0

    lax.fori_loop(0, 18, plane_v, 0)

    for x in range(WX):
        for c, value in enumerate(step(v_ref, x + 1, x + 2, 0)):
            out[c, pl.ds(x, NZ, stride=WX), :] = value


def whole(count):
    return [pl.BlockSpec(memory_space=pltpu.VMEM)] * count


def on_device(frames, trailing):
    own = frames[0]
    n_ta, n_gx, n_gy = (lax.axis_size(a) for a in ("ta", "gx", "gy"))

    def passed(value, axis, step):
        count = lax.axis_size(axis)
        pairs = [(i, i + step) for i in range(count) if 0 <= i + step < count]
        return lax.ppermute(value, axis, pairs)

    arriving = passed(own, "ta", -1)
    nxt = jnp.where(lax.axis_index("ta") == n_ta - 1, trailing, arriving)
    low = passed(jnp.stack([own[:, WX - EDGE :], nxt[:, WX - EDGE :]]), "gx", 1)
    high = passed(jnp.stack([own[:, :EDGE], nxt[:, :EDGE]]), "gx", -1)
    message = jax.ShapeDtypeStruct((128, 128), BF16)
    to_right, to_left = pl.pallas_call(
        pack_kernel, out_shape=(message, message), in_specs=whole(4), out_specs=tuple(whole(2)), name="pack"
    )(own, nxt, low, high)
    from_left, from_right = passed(to_right, "gy", 1), passed(to_left, "gy", -1)
    plane = (NZ, LANES)
    flow = pl.pallas_call(
        flow_kernel,
        out_shape=jax.ShapeDtypeStruct((3, NZ * WX, LANES), F32),
        in_specs=whole(6),
        out_specs=whole(1)[0],
        scratch_shapes=[
            pltpu.VMEM((2, 32 * NZ, LANES), F32),
            pltpu.VMEM((2, 32 * NZ, LANES), F32),
            pltpu.VMEM((2, 22) + plane, F32),
            pltpu.VMEM((2, 22) + plane, F32),
            pltpu.VMEM((4, 2, 20) + plane, F32),
            pltpu.VMEM((3, 2, 20) + plane, F32),
            pltpu.VMEM((3, 2, 18) + plane, F32),
        ],
        name="flow",
    )(own, nxt, low, high, from_left, from_right)
    return flow.reshape(1, 3, NZ, WX, LANES)


def solution(mesh):
    return jax.shard_map(
        on_device,
        mesh=mesh,
        in_specs=(P("ta", None, "gx", "gy"), P(None, "gx", "gy")),
        out_specs=P("ta", None, None, "gx", "gy"),
        check_vma=False,
    )
```

```python
import jax
import jax.numpy as jnp
from jax import lax
from jax.experimental import pallas as pl
from jax.experimental.pallas import tpu as pltpu
from jax.sharding import PartitionSpec as P

NZ = 32
WX = 16
WY = 128
EDGE = 8
PITCH = 40
F32, BF16 = jnp.float32, jnp.bfloat16


def iota(shape, dim):
    return lax.broadcasted_iota(jnp.int32, shape, dim)


def dot(a, b):
    return jnp.dot(a, b, preferred_element_type=F32)


def y_taps(distance):
    d = jnp.abs(distance)
    tap = jnp.where(d == 0, 6.0, jnp.where(d == 1, 4.0, jnp.where(d == 2, 1.0, 0.0)))
    return tap * (1.0 / 4096.0)


def octet_rows(source, z_half):
    return source[16 * z_half : 16 * z_half + 16].astype(F32).reshape(128, WY).astype(BF16)


def strip_column(lane):
    place = lane & 31
    return jnp.where(place < 16, place - 5, place + 101)


def edge_columns(blocks):
    row, lane = iota((WY, 256), 0), iota((WY, 256), 1)
    column = (lane & 7) + jnp.where(lane < 128, WY - EDGE, 0)
    pick = jnp.where(row == column, 1.0, 0.0).astype(BF16)
    group = (iota((128, 256), 1) & 127) >> 3
    packed = jnp.zeros((128, 256), F32)
    for (octet, frame), block in blocks.items():
        for z_half in range(2):
            found = dot(octet_rows(block, z_half), pick)
            packed = jnp.where(group == (octet * 2 + frame) * 2 + z_half, found, packed)
    return packed.astype(BF16)


def pack_own_kernel(own, nxt, packed):
    packed[...] = edge_columns(
        {
            (octet, frame): block[:, 8 * octet - 8 : 8 * octet, :]
            for octet in (1, 2)
            for frame, block in enumerate((own, nxt))
        }
    )


def pack_rim_kernel(low, high, packed, to_right, to_left):
    rim = edge_columns(
        {(octet, frame): block[frame] for octet, block in ((0, low), (3, high)) for frame in range(2)}
    )
    both = packed[...] + rim
    to_right[...] = both[:, :128]
    to_left[...] = both[:, 128:]


class Planes:
    def __init__(self, ref, index=None):
        self.ref, self.index = ref, index

    def rows(self, start, count, stride=None):
        rows = pl.ds(start, count) if stride is None else pl.ds(start, count, stride=stride)
        return (rows, slice(None)) if self.index is None else (self.index, rows, slice(None))

    def get(self, plane, shift=0):
        return self.ref[self.rows(8 + PITCH * plane + shift, NZ)]

    def put(self, plane, value):
        self.ref[self.rows(8 + PITCH * plane, NZ)] = value

    def put_z(self, plane, z, values):
        self.ref[self.rows(8 + PITCH * plane + z, values.shape[0], PITCH)] = values

    def clear(self, first, last):
        for plane in range(first, last + 2):
            self.ref[self.rows(PITCH * plane, 8)] = jnp.zeros((8, WY), F32)


def planes_of(count):
    return pltpu.VMEM((8 + PITCH * count, WY), F32)


def planes_of_3(count):
    return pltpu.VMEM((3, 8 + PITCH * count, WY), F32)


def smooth_z(planes, k):
    near = planes.get(k, 1) + planes.get(k, -1)
    far = planes.get(k, 2) + planes.get(k, -2)
    return 6.0 * planes.get(k) + 4.0 * near + far


def smooth_x(planes, k):
    near = planes.get(k + 1) + planes.get(k - 1)
    far = planes.get(k + 2) + planes.get(k - 2)
    return 6.0 * planes.get(k) + 4.0 * near + far


def y_pair(v):
    return pltpu.roll(v, WY - 1, 1), pltpu.roll(v, 1, 1)


def gradient_terms(s, k, change):
    y_next, y_prev = y_pair(s.get(k))
    grads = (s.get(k + 1) - s.get(k - 1), y_next - y_prev, s.get(k, 1) - s.get(k, -1))
    denom = 0.01 + grads[0] * grads[0] + grads[1] * grads[1] + grads[2] * grads[2]
    scale = lax.rsqrt(denom)
    scale = scale * (1.5 - 0.5 * denom * scale * scale)
    return [grad * scale for grad in grads], change * scale


def jacobi(velocity, k, terms):
    means = []
    for planes in velocity:
        y_next, y_prev = y_pair(planes.get(k))
        total = (planes.get(k + 1) + planes.get(k - 1)) + (y_next + y_prev)
        total = total + (planes.get(k, 1) + planes.get(k, -1))
        means.append(total * (1.0 / 6.0))
    common = terms[3] + terms[0] * means[0] + terms[1] * means[1] + terms[2] * means[2]
    return [mean - term * common for mean, term in zip(means, terms)]


def inside():
    faces = []
    for axis in ("gx", "gy"):
        at = lax.axis_index(axis)
        faces += [jnp.where(at == 0, 0.0, 1.0), jnp.where(at == lax.axis_size(axis) - 1, 0.0, 1.0)]
    return faces


def inner_kernel(own, nxt, low, high, inner, part, edge_taps, p_ref, q_ref, s_ref, c_ref, h_ref, u_ref, v_ref):
    x_low, x_high, _, _ = inside()

    def weight(x):
        return x_low if x < 0 else x_high if x >= WX else None

    def weighed(value, x):
        return value if weight(x) is None else value * weight(x)

    p, q, s = Planes(p_ref), Planes(q_ref), Planes(s_ref)
    u, v = [Planes(u_ref, c) for c in range(3)], [Planes(v_ref, c) for c in range(3)]
    p.clear(3, 28)
    q.clear(3, 28)
    s.clear(1, 20)
    for c in range(3):
        u[c].clear(1, 18)
        v[c].clear(1, 16)

    row, lane = iota((WY, WY), 0), iota((WY, WY), 1)
    taps = y_taps(lane - row).astype(BF16)
    strip_taps = y_taps(strip_column(lane) - row)
    octet_taps = jnp.concatenate(
        [jnp.where((lane >> 5) == octet, strip_taps, 0.0) for octet in range(4)], axis=0
    ).astype(BF16)

    row, lane = iota((256, WY), 0), iota((256, WY), 1)
    column = (row & 7) + jnp.where(row < 128, -EDGE, WY)
    edge = jnp.where(((row & 127) >> 5) == (lane >> 5), y_taps(strip_column(lane) - column), 0.0)
    for group in range(4):
        edge_taps[group] = jnp.where(((row >> 3) & 3) == group, edge, 0.0).astype(BF16)

    for z_half in range(2):
        octets = [[], []]
        for octet in range(4):
            found = []
            for frame, centre in enumerate((own, nxt)):
                block = (
                    (low if octet == 0 else high)[frame, 16 * z_half : 16 * z_half + 16]
                    if octet in (0, 3)
                    else centre[16 * z_half : 16 * z_half + 16, 8 * octet - 8 : 8 * octet, :]
                )
                rows = block.astype(F32).reshape(128, WY).astype(BF16)
                octets[frame].append(rows)
                found.append(dot(rows, taps))
            total, change = (found[0] + found[1]) * 0.25, found[1] - found[0]
            for i in range(16):
                p.put_z(8 * octet, 16 * z_half + i, total[8 * i : 8 * i + 8])
                q.put_z(8 * octet, 16 * z_half + i, change[8 * i : 8 * i + 8])
        for frame in range(2):
            part[frame, z_half] = dot(jnp.concatenate(octets[frame], axis=1), octet_taps)

    for k in range(3, 29):
        p.put(k, smooth_z(p, k))
        q.put(k, smooth_z(q, k))
    for k in range(22):
        s.put(k, weighed(smooth_x(p, k + 5), k - 3))
        if 1 <= k <= 20:
            c_ref[k - 1] = weighed(smooth_x(q, k + 5), k - 3)

    for k in range(20):
        terms, change = gradient_terms(s, k + 1, c_ref[k])
        h_ref[3, k] = change
        for c in range(3):
            h_ref[c, k] = terms[c]
            u[c].put(k, -terms[c] * change)

    for k in range(18):
        for c, value in enumerate(jacobi(u, k + 1, [h_ref[c, k + 1] for c in range(4)])):
            v[c].put(k, weighed(value, k - 1))
    for x in range(WX):
        for c, value in enumerate(jacobi(v, x + 1, [h_ref[c, x + 2] for c in range(4)])):
            inner[c, x] = value


def strip_kernel(inner, part, edge_taps, from_left, from_right, out, p_ref, q_ref, s_ref, c_ref, h_ref, u_ref, v_ref):
    x_low, x_high, y_low, y_high = inside()
    lane = iota((1, WY), 1)
    column = strip_column(lane)
    weight = (
        jnp.where(lane < 32, x_low, 1.0)
        * jnp.where(lane >= 96, x_high, 1.0)
        * jnp.where(column < 0, y_low, 1.0)
        * jnp.where(column >= WY, y_high, 1.0)
    )
    p, q, s = Planes(p_ref), Planes(q_ref), Planes(s_ref)
    u, v = [Planes(u_ref, c) for c in range(3)], [Planes(v_ref, c) for c in range(3)]
    for planes, first in [(p, 2), (q, 2), (s, 1)] + [(planes, 1) for planes in u + v]:
        planes.clear(first, first + 7)

    def put(planes, i, value, rim):
        planes.put(i + rim, value)
        if i < rim:
            planes.put(i + rim + 8, pltpu.roll(value, 96, 1))
        if i >= 8 - rim:
            planes.put(i + rim - 8, pltpu.roll(value, 32, 1))

    edges = jnp.concatenate([from_left[...], from_right[...]], axis=1)
    for z_half in range(2):
        found = [part[frame, z_half] + dot(edges, edge_taps[2 * frame + z_half]) for frame in range(2)]
        total, change = (found[0] + found[1]) * 0.25, found[1] - found[0]
        for i in range(16):
            p.put_z(2, 16 * z_half + i, total[8 * i : 8 * i + 8])
            q.put_z(2, 16 * z_half + i, change[8 * i : 8 * i + 8])
    for i in range(8):
        put(p, i, smooth_z(p, i + 2), 2)
        put(q, i, smooth_z(q, i + 2), 2)
    for i in range(8):
        put(s, i, smooth_x(p, i + 2) * weight, 1)
        c_ref[i] = smooth_x(q, i + 2) * weight
    for i in range(8):
        terms, change = gradient_terms(s, i + 1, c_ref[i])
        h_ref[3, i] = change
        for c in range(3):
            h_ref[c, i] = terms[c]
            put(u[c], i, -terms[c] * change, 1)
    for i in range(8):
        for c, value in enumerate(jacobi(u, i + 1, [h_ref[c, i] for c in range(4)])):
            put(v[c], i, value * weight, 1)
    own_lane = iota((NZ, WY), 1)
    rim = (own_lane < 5) | (own_lane >= WY - 5)
    for i in range(8):
        for c, value in enumerate(jacobi(v, i + 1, [h_ref[c, i] for c in range(4)])):
            value = jnp.where((own_lane & 31) < 5, pltpu.roll(value, WY - 22, 1), value)
            for half in range(2):
                x = 8 * half + i
                placed = pltpu.roll(value, WY - 32 * (half + 1) - 5, 1)
                out[c, pl.ds(x, NZ, stride=WX), :] = jnp.where(rim, placed, inner[c, x])


def call(kernel, outs, args, scratch, megabytes, flops, name):
    moved = sum(a.size * a.dtype.itemsize for a in (*args, *outs))
    spec = pl.BlockSpec(memory_space=pltpu.VMEM)
    return pl.pallas_call(
        kernel,
        out_shape=outs,
        in_specs=[spec] * len(args),
        out_specs=tuple([spec] * len(outs)),
        scratch_shapes=scratch,
        compiler_params=pltpu.CompilerParams(vmem_limit_bytes=megabytes << 20),
        cost_estimate=pl.CostEstimate(flops=flops, bytes_accessed=moved, transcendentals=0),
        name=name,
    )(*args)


def shape(*dims, dtype=F32):
    return jax.ShapeDtypeStruct(dims, dtype)


def on_device(frames, trailing):
    own = frames[0]

    def passed(value, axis, step):
        count = lax.axis_size(axis)
        pairs = [(i, i + step) for i in range(count) if 0 <= i + step < count]
        return lax.ppermute(value, axis, pairs)

    arriving = passed(own, "ta", -1)
    nxt = jnp.where(lax.axis_index("ta") == lax.axis_size("ta") - 1, trailing, arriving)
    low = passed(jnp.stack([own[:, WX - EDGE :], nxt[:, WX - EDGE :]]), "gx", 1)
    high = passed(jnp.stack([own[:, :EDGE], nxt[:, :EDGE]]), "gx", -1)
    (packed,) = call(
        pack_own_kernel, (shape(128, 256, dtype=BF16),), (own, nxt), [], 8, 10**8, "pack_own"
    )
    message = shape(128, 128, dtype=BF16)
    to_right, to_left = call(
        pack_rim_kernel, (message, message), (low, high, packed), [], 8, 10**8, "pack_rim"
    )
    from_left, from_right = passed(to_right, "gy", 1), passed(to_left, "gy", -1)
    inner, part, edge_taps = call(
        inner_kernel,
        (shape(3, WX, NZ, WY), shape(2, 2, 128, WY), shape(4, 256, WY, dtype=BF16)),
        (own, nxt, low, high),
        [
            planes_of(32),
            planes_of(32),
            planes_of(22),
            pltpu.VMEM((20, NZ, WY), F32),
            pltpu.VMEM((4, 20, NZ, WY), F32),
            planes_of_3(20),
            planes_of_3(18),
        ],
        16,
        10**9,
        "inner",
    )
    (flow,) = call(
        strip_kernel,
        (shape(3, NZ * WX, WY),),
        (inner, part, edge_taps, from_left, from_right),
        [
            planes_of(12),
            planes_of(12),
            planes_of(10),
            pltpu.VMEM((8, NZ, WY), F32),
            pltpu.VMEM((4, 8, NZ, WY), F32),
            planes_of_3(10),
            planes_of_3(10),
        ],
        16,
        10**8,
        "strip",
    )
    return flow.reshape(1, 3, NZ, WX, WY)


def solution(mesh):
    return jax.shard_map(
        on_device,
        mesh=mesh,
        in_specs=(P("ta", None, "gx", "gy"), P(None, "gx", "gy")),
        out_specs=P("ta", None, None, "gx", "gy"),
        check_vma=False,
    )
```

```python
import jax
import jax.numpy as jnp
from jax import lax
from jax.experimental import pallas as pl
from jax.experimental.pallas import tpu as pltpu
from jax.sharding import PartitionSpec as P

NZ = 32
WX = 16
WY = 128
EDGE = 8
PITCH = 40
F32, BF16 = jnp.float32, jnp.bfloat16


def iota(shape, dim):
    return lax.broadcasted_iota(jnp.int32, shape, dim)


def dot(a, b):
    return jnp.dot(a, b, preferred_element_type=F32)


def y_taps(distance):
    d = jnp.abs(distance)
    tap = jnp.where(d == 0, 6.0, jnp.where(d == 1, 4.0, jnp.where(d == 2, 1.0, 0.0)))
    return tap * (1.0 / 4096.0)


def octet_rows(source, z_half):
    return source[16 * z_half : 16 * z_half + 16].astype(F32).reshape(128, WY).astype(BF16)


def strip_column(lane):
    place = lane & 31
    return jnp.where(place < 16, place - 5, place + 101)


def edge_columns(blocks):
    row, lane = iota((WY, 256), 0), iota((WY, 256), 1)
    column = (lane & 7) + jnp.where(lane < 128, WY - EDGE, 0)
    pick = jnp.where(row == column, 1.0, 0.0).astype(BF16)
    group = (iota((128, 256), 1) & 127) >> 3
    packed = jnp.zeros((128, 256), F32)
    for (octet, frame), block in blocks.items():
        for z_half in range(2):
            found = dot(octet_rows(block, z_half), pick)
            packed = jnp.where(group == (octet * 2 + frame) * 2 + z_half, found, packed)
    return packed.astype(BF16)


def pack_own_kernel(own, nxt, packed):
    packed[...] = edge_columns(
        {
            (octet, frame): block[:, 8 * octet - 8 : 8 * octet, :]
            for octet in (1, 2)
            for frame, block in enumerate((own, nxt))
        }
    )


def pack_rim_kernel(low, high, packed, to_right, to_left):
    rim = edge_columns(
        {(octet, frame): block[frame] for octet, block in ((0, low), (3, high)) for frame in range(2)}
    )
    both = packed[...] + rim
    to_right[...] = both[:, :128]
    to_left[...] = both[:, 128:]


class Planes:
    def __init__(self, ref, index=None):
        self.ref, self.index = ref, index

    def rows(self, start, count, stride=None):
        rows = pl.ds(start, count) if stride is None else pl.ds(start, count, stride=stride)
        return (rows, slice(None)) if self.index is None else (self.index, rows, slice(None))

    def get(self, plane, shift=0):
        return self.ref[self.rows(8 + PITCH * plane + shift, NZ)]

    def put(self, plane, value):
        self.ref[self.rows(8 + PITCH * plane, NZ)] = value

    def put_z(self, plane, z, values):
        self.ref[self.rows(8 + PITCH * plane + z, values.shape[0], PITCH)] = values

    def clear(self, first, last):
        for plane in range(first, last + 2):
            self.ref[self.rows(PITCH * plane, 8)] = jnp.zeros((8, WY), F32)


def planes_of(count):
    return pltpu.VMEM((8 + PITCH * count, WY), F32)


def planes_of_3(count):
    return pltpu.VMEM((3, 8 + PITCH * count, WY), F32)


def smooth_z(planes, k):
    near = planes.get(k, 1) + planes.get(k, -1)
    far = planes.get(k, 2) + planes.get(k, -2)
    return 6.0 * planes.get(k) + 4.0 * near + far


def smooth_x(planes, k):
    near = planes.get(k + 1) + planes.get(k - 1)
    far = planes.get(k + 2) + planes.get(k - 2)
    return 6.0 * planes.get(k) + 4.0 * near + far


def y_pair(v):
    return pltpu.roll(v, WY - 1, 1), pltpu.roll(v, 1, 1)


def gradient_terms(s, k, change):
    y_next, y_prev = y_pair(s.get(k))
    grads = (s.get(k + 1) - s.get(k - 1), y_next - y_prev, s.get(k, 1) - s.get(k, -1))
    denom = 0.01 + grads[0] * grads[0] + grads[1] * grads[1] + grads[2] * grads[2]
    scale = lax.rsqrt(denom)
    scale = scale * (1.5 - 0.5 * denom * scale * scale)
    return [grad * scale for grad in grads], change * scale


def jacobi(velocity, k, terms):
    means = []
    for planes in velocity:
        y_next, y_prev = y_pair(planes.get(k))
        total = (planes.get(k + 1) + planes.get(k - 1)) + (y_next + y_prev)
        total = total + (planes.get(k, 1) + planes.get(k, -1))
        means.append(total * (1.0 / 6.0))
    common = terms[3] + terms[0] * means[0] + terms[1] * means[1] + terms[2] * means[2]
    return [mean - term * common for mean, term in zip(means, terms)]


def inside():
    faces = []
    for axis in ("gx", "gy"):
        at = lax.axis_index(axis)
        faces += [jnp.where(at == 0, 0.0, 1.0), jnp.where(at == lax.axis_size(axis) - 1, 0.0, 1.0)]
    return faces


def inner_kernel(own, nxt, low, high, inner, part, edge_taps, p_ref, q_ref, s_ref, c_ref, h_ref, u_ref, v_ref):
    x_low, x_high, _, _ = inside()

    def weight(x):
        return x_low if x < 0 else x_high if x >= WX else None

    def weighed(value, x):
        return value if weight(x) is None else value * weight(x)

    p, q, s = Planes(p_ref), Planes(q_ref), Planes(s_ref)
    u, v = [Planes(u_ref, c) for c in range(3)], [Planes(v_ref, c) for c in range(3)]
    p.clear(3, 28)
    q.clear(3, 28)
    s.clear(1, 20)
    for c in range(3):
        u[c].clear(1, 18)
        v[c].clear(1, 16)

    row, lane = iota((WY, WY), 0), iota((WY, WY), 1)
    taps = y_taps(lane - row).astype(BF16)
    strip_taps = y_taps(strip_column(lane) - row)
    octet_taps = jnp.concatenate(
        [jnp.where((lane >> 5) == octet, strip_taps, 0.0) for octet in range(4)], axis=0
    ).astype(BF16)

    row, lane = iota((256, WY), 0), iota((256, WY), 1)
    column = (row & 7) + jnp.where(row < 128, -EDGE, WY)
    edge = jnp.where(((row & 127) >> 5) == (lane >> 5), y_taps(strip_column(lane) - column), 0.0)
    for group in range(4):
        edge_taps[group] = jnp.where(((row >> 3) & 3) == group, edge, 0.0).astype(BF16)

    for z_half in range(2):
        octets = [[], []]
        for octet in range(4):
            found = []
            for frame, centre in enumerate((own, nxt)):
                block = (
                    (low if octet == 0 else high)[frame, 16 * z_half : 16 * z_half + 16]
                    if octet in (0, 3)
                    else centre[16 * z_half : 16 * z_half + 16, 8 * octet - 8 : 8 * octet, :]
                )
                rows = block.astype(F32).reshape(128, WY).astype(BF16)
                octets[frame].append(rows)
                found.append(dot(rows, taps))
            total, change = (found[0] + found[1]) * 0.25, found[1] - found[0]
            for i in range(16):
                p.put_z(8 * octet, 16 * z_half + i, total[8 * i : 8 * i + 8])
                q.put_z(8 * octet, 16 * z_half + i, change[8 * i : 8 * i + 8])
        for frame in range(2):
            part[frame, z_half] = dot(jnp.concatenate(octets[frame], axis=1), octet_taps)

    for k in range(3, 29):
        p.put(k, smooth_z(p, k))
        q.put(k, smooth_z(q, k))
    for k in range(22):
        s.put(k, weighed(smooth_x(p, k + 5), k - 3))
        if 1 <= k <= 20:
            c_ref[k - 1] = weighed(smooth_x(q, k + 5), k - 3)

    for k in range(20):
        terms, change = gradient_terms(s, k + 1, c_ref[k])
        h_ref[3, k] = change
        for c in range(3):
            h_ref[c, k] = terms[c]
            u[c].put(k, -terms[c] * change)

    for k in range(18):
        for c, value in enumerate(jacobi(u, k + 1, [h_ref[c, k + 1] for c in range(4)])):
            v[c].put(k, weighed(value, k - 1))
    for x in range(WX):
        for c, value in enumerate(jacobi(v, x + 1, [h_ref[c, x + 2] for c in range(4)])):
            inner[c, x] = value


def strip_kernel(inner, part, edge_taps, from_left, from_right, out, p_ref, q_ref, s_ref, c_ref, h_ref, u_ref, v_ref):
    x_low, x_high, y_low, y_high = inside()
    lane = iota((1, WY), 1)
    column = strip_column(lane)
    weight = (
        jnp.where(lane < 32, x_low, 1.0)
        * jnp.where(lane >= 96, x_high, 1.0)
        * jnp.where(column < 0, y_low, 1.0)
        * jnp.where(column >= WY, y_high, 1.0)
    )
    p, q, s = Planes(p_ref), Planes(q_ref), Planes(s_ref)
    u, v = [Planes(u_ref, c) for c in range(3)], [Planes(v_ref, c) for c in range(3)]
    for planes, first in [(p, 2), (q, 2), (s, 1)] + [(planes, 1) for planes in u + v]:
        planes.clear(first, first + 7)

    def put(planes, i, value, rim):
        planes.put(i + rim, value)
        if i < rim:
            planes.put(i + rim + 8, pltpu.roll(value, 96, 1))
        if i >= 8 - rim:
            planes.put(i + rim - 8, pltpu.roll(value, 32, 1))

    edges = jnp.concatenate([from_left[...], from_right[...]], axis=1)
    for z_half in range(2):
        found = [part[frame, z_half] + dot(edges, edge_taps[2 * frame + z_half]) for frame in range(2)]
        total, change = (found[0] + found[1]) * 0.25, found[1] - found[0]
        for i in range(16):
            p.put_z(2, 16 * z_half + i, total[8 * i : 8 * i + 8])
            q.put_z(2, 16 * z_half + i, change[8 * i : 8 * i + 8])
    for i in range(8):
        put(p, i, smooth_z(p, i + 2), 2)
        put(q, i, smooth_z(q, i + 2), 2)
    for i in range(8):
        put(s, i, smooth_x(p, i + 2) * weight, 1)
        c_ref[i] = smooth_x(q, i + 2) * weight
    for i in range(8):
        terms, change = gradient_terms(s, i + 1, c_ref[i])
        h_ref[3, i] = change
        for c in range(3):
            h_ref[c, i] = terms[c]
            put(u[c], i, -terms[c] * change, 1)
    for i in range(8):
        for c, value in enumerate(jacobi(u, i + 1, [h_ref[c, i] for c in range(4)])):
            put(v[c], i, value * weight, 1)
    own_lane = iota((NZ, WY), 1)
    rim = (own_lane < 5) | (own_lane >= WY - 5)
    for i in range(8):
        for c, value in enumerate(jacobi(v, i + 1, [h_ref[c, i] for c in range(4)])):
            value = jnp.where((own_lane & 31) < 5, pltpu.roll(value, WY - 22, 1), value)
            for half in range(2):
                x = 8 * half + i
                placed = pltpu.roll(value, WY - 32 * (half + 1) - 5, 1)
                out[c, pl.ds(x, NZ, stride=WX), :] = jnp.where(rim, placed, inner[c, x])


def call(kernel, outs, args, scratch, megabytes, flops, name):
    moved = sum(a.size * a.dtype.itemsize for a in (*args, *outs))
    spec = pl.BlockSpec(memory_space=pltpu.VMEM)
    return pl.pallas_call(
        kernel,
        out_shape=outs,
        in_specs=[spec] * len(args),
        out_specs=tuple([spec] * len(outs)),
        scratch_shapes=scratch,
        compiler_params=pltpu.CompilerParams(vmem_limit_bytes=megabytes << 20),
        cost_estimate=pl.CostEstimate(flops=flops, bytes_accessed=moved, transcendentals=0),
        name=name,
    )(*args)


def shape(*dims, dtype=F32):
    return jax.ShapeDtypeStruct(dims, dtype)


def on_device(frames, trailing):
    own = frames[0]

    def passed(value, axis, step):
        count = lax.axis_size(axis)
        pairs = [(i, i + step) for i in range(count) if 0 <= i + step < count]
        return lax.ppermute(value, axis, pairs)

    def swapped(value, axis, first):
        pairs = [(i, i + 1) for i in range(first, lax.axis_size(axis) - 1, 2)]
        return lax.ppermute(value, axis, pairs + [(b, a) for a, b in pairs])

    arriving = passed(own, "ta", -1)
    nxt = jnp.where(lax.axis_index("ta") == lax.axis_size("ta") - 1, trailing, arriving)
    upper, lower = jnp.stack([own[:, WX - EDGE :], nxt[:, WX - EDGE :]]), jnp.stack([own[:, :EDGE], nxt[:, :EDGE]])
    even = lax.axis_index("gx") % 2 == 0
    on_chip = swapped(jnp.where(even, upper, lower), "gx", 0)
    off_chip = swapped(jnp.where(even, lower, upper), "gx", 1)
    low, high = jnp.where(even, off_chip, on_chip), jnp.where(even, on_chip, off_chip)
    (packed,) = call(
        pack_own_kernel, (shape(128, 256, dtype=BF16),), (own, nxt), [], 8, 10**8, "pack_own"
    )
    message = shape(128, 128, dtype=BF16)
    to_right, to_left = call(
        pack_rim_kernel, (message, message), (low, high, packed), [], 8, 10**8, "pack_rim"
    )
    from_left, from_right = passed(to_right, "gy", 1), passed(to_left, "gy", -1)
    inner, part, edge_taps = call(
        inner_kernel,
        (shape(3, WX, NZ, WY), shape(2, 2, 128, WY), shape(4, 256, WY, dtype=BF16)),
        (own, nxt, low, high),
        [
            planes_of(32),
            planes_of(32),
            planes_of(22),
            pltpu.VMEM((20, NZ, WY), F32),
            pltpu.VMEM((4, 20, NZ, WY), F32),
            planes_of_3(20),
            planes_of_3(18),
        ],
        16,
        10**9,
        "inner",
    )
    (flow,) = call(
        strip_kernel,
        (shape(3, NZ * WX, WY),),
        (inner, part, edge_taps, from_left, from_right),
        [
            planes_of(12),
            planes_of(12),
            planes_of(10),
            pltpu.VMEM((8, NZ, WY), F32),
            pltpu.VMEM((4, 8, NZ, WY), F32),
            planes_of_3(10),
            planes_of_3(10),
        ],
        16,
        10**8,
        "strip",
    )
    return flow.reshape(1, 3, NZ, WX, WY)


def solution(mesh):
    return jax.shard_map(
        on_device,
        mesh=mesh,
        in_specs=(P("ta", None, "gx", "gy"), P(None, "gx", "gy")),
        out_specs=P("ta", None, None, "gx", "gy"),
        check_vma=False,
    )
```

```python
import jax
import jax.numpy as jnp
from jax import lax
from jax.experimental import pallas as pl
from jax.experimental.pallas import tpu as pltpu
from jax.sharding import PartitionSpec as P

NZ = 32
WX = 16
WY = 128
EDGE = 8
PITCH = 40
F32, BF16 = jnp.float32, jnp.bfloat16


def iota(shape, dim):
    return lax.broadcasted_iota(jnp.int32, shape, dim)


def dot(a, b):
    return jnp.dot(a, b, preferred_element_type=F32)


def y_taps(distance):
    d = jnp.abs(distance)
    tap = jnp.where(d == 0, 6.0, jnp.where(d == 1, 4.0, jnp.where(d == 2, 1.0, 0.0)))
    return tap * (1.0 / 4096.0)


def octet_rows(source, z_half):
    return source[16 * z_half : 16 * z_half + 16].astype(F32).reshape(128, WY).astype(BF16)


def strip_column(lane):
    place = lane & 31
    return jnp.where(place < 16, place - 5, place + 101)


def edge_columns(blocks):
    row, lane = iota((WY, 256), 0), iota((WY, 256), 1)
    column = (lane & 7) + jnp.where(lane < 128, WY - EDGE, 0)
    pick = jnp.where(row == column, 1.0, 0.0).astype(BF16)
    group = (iota((128, 256), 1) & 127) >> 3
    packed = jnp.zeros((128, 256), F32)
    for (octet, frame), block in blocks.items():
        for z_half in range(2):
            found = dot(octet_rows(block, z_half), pick)
            packed = jnp.where(group == (octet * 2 + frame) * 2 + z_half, found, packed)
    return packed.astype(BF16)


def pack_own_kernel(own, nxt, packed):
    packed[...] = edge_columns(
        {
            (octet, frame): block[:, 8 * octet - 8 : 8 * octet, :]
            for octet in (1, 2)
            for frame, block in enumerate((own, nxt))
        }
    )


def pack_rim_kernel(low, high, packed, to_right, to_left):
    rim = edge_columns(
        {(octet, frame): block[frame] for octet, block in ((0, low), (3, high)) for frame in range(2)}
    )
    both = packed[...] + rim
    to_right[...] = both[:, :128]
    to_left[...] = both[:, 128:]


class Planes:
    def __init__(self, ref, index=None):
        self.ref, self.index = ref, index

    def rows(self, start, count, stride=None):
        rows = pl.ds(start, count) if stride is None else pl.ds(start, count, stride=stride)
        return (rows, slice(None)) if self.index is None else (self.index, rows, slice(None))

    def get(self, plane, shift=0):
        return self.ref[self.rows(8 + PITCH * plane + shift, NZ)]

    def put(self, plane, value):
        self.ref[self.rows(8 + PITCH * plane, NZ)] = value

    def put_z(self, plane, z, values):
        self.ref[self.rows(8 + PITCH * plane + z, values.shape[0], PITCH)] = values

    def clear(self, first, last):
        for plane in range(first, last + 2):
            self.ref[self.rows(PITCH * plane, 8)] = jnp.zeros((8, WY), F32)


def planes_of(count):
    return pltpu.VMEM((8 + PITCH * count, WY), F32)


def planes_of_3(count):
    return pltpu.VMEM((3, 8 + PITCH * count, WY), F32)


def smooth_z(planes, k):
    near = planes.get(k, 1) + planes.get(k, -1)
    far = planes.get(k, 2) + planes.get(k, -2)
    return 6.0 * planes.get(k) + 4.0 * near + far


def smooth_x(planes, k):
    near = planes.get(k + 1) + planes.get(k - 1)
    far = planes.get(k + 2) + planes.get(k - 2)
    return 6.0 * planes.get(k) + 4.0 * near + far


def y_pair(v):
    return pltpu.roll(v, WY - 1, 1), pltpu.roll(v, 1, 1)


def gradient_terms(s, k, change):
    y_next, y_prev = y_pair(s.get(k))
    grads = (s.get(k + 1) - s.get(k - 1), y_next - y_prev, s.get(k, 1) - s.get(k, -1))
    denom = 0.01 + grads[0] * grads[0] + grads[1] * grads[1] + grads[2] * grads[2]
    scale = lax.rsqrt(denom)
    scale = scale * (1.5 - 0.5 * denom * scale * scale)
    return [grad * scale for grad in grads], change * scale


def jacobi(velocity, k, terms):
    means = []
    for planes in velocity:
        y_next, y_prev = y_pair(planes.get(k))
        total = (planes.get(k + 1) + planes.get(k - 1)) + (y_next + y_prev)
        total = total + (planes.get(k, 1) + planes.get(k, -1))
        means.append(total * (1.0 / 6.0))
    common = terms[3] + terms[0] * means[0] + terms[1] * means[1] + terms[2] * means[2]
    return [mean - term * common for mean, term in zip(means, terms)]


def inside():
    faces = []
    for axis in ("gx", "gy"):
        at = lax.axis_index(axis)
        faces += [jnp.where(at == 0, 0.0, 1.0), jnp.where(at == lax.axis_size(axis) - 1, 0.0, 1.0)]
    return faces


def inner_kernel(own, nxt, low, high, inner, part, edge_taps, p_ref, q_ref, s_ref, c_ref, h_ref, u_ref, v_ref):
    x_low, x_high, _, _ = inside()

    def weight(x):
        return x_low if x < 0 else x_high if x >= WX else None

    def weighed(value, x):
        return value if weight(x) is None else value * weight(x)

    p, q, s = Planes(p_ref), Planes(q_ref), Planes(s_ref)
    u, v = [Planes(u_ref, c) for c in range(3)], [Planes(v_ref, c) for c in range(3)]
    p.clear(3, 28)
    q.clear(3, 28)
    s.clear(1, 20)
    for c in range(3):
        u[c].clear(1, 18)
        v[c].clear(1, 16)

    row, lane = iota((WY, WY), 0), iota((WY, WY), 1)
    taps = y_taps(lane - row).astype(BF16)
    strip_taps = y_taps(strip_column(lane) - row)
    octet_taps = jnp.concatenate(
        [jnp.where((lane >> 5) == octet, strip_taps, 0.0) for octet in range(4)], axis=0
    ).astype(BF16)

    row, lane = iota((256, WY), 0), iota((256, WY), 1)
    column = (row & 7) + jnp.where(row < 128, -EDGE, WY)
    edge = jnp.where(((row & 127) >> 5) == (lane >> 5), y_taps(strip_column(lane) - column), 0.0)
    for group in range(4):
        edge_taps[group] = jnp.where(((row >> 3) & 3) == group, edge, 0.0).astype(BF16)

    for z_half in range(2):
        octets = [[], []]
        for octet in range(4):
            found = []
            for frame, centre in enumerate((own, nxt)):
                block = (
                    (low if octet == 0 else high)[frame, 16 * z_half : 16 * z_half + 16]
                    if octet in (0, 3)
                    else centre[16 * z_half : 16 * z_half + 16, 8 * octet - 8 : 8 * octet, :]
                )
                rows = block.astype(F32).reshape(128, WY).astype(BF16)
                octets[frame].append(rows)
                found.append(dot(rows, taps))
            total, change = (found[0] + found[1]) * 0.25, found[1] - found[0]
            for i in range(16):
                p.put_z(8 * octet, 16 * z_half + i, total[8 * i : 8 * i + 8])
                q.put_z(8 * octet, 16 * z_half + i, change[8 * i : 8 * i + 8])
        for frame in range(2):
            part[frame, z_half] = dot(jnp.concatenate(octets[frame], axis=1), octet_taps)

    for k in range(3, 29):
        p.put(k, smooth_z(p, k))
        q.put(k, smooth_z(q, k))
    for k in range(22):
        s.put(k, weighed(smooth_x(p, k + 5), k - 3))
        if 1 <= k <= 20:
            c_ref[k - 1] = weighed(smooth_x(q, k + 5), k - 3)

    for k in range(20):
        terms, change = gradient_terms(s, k + 1, c_ref[k])
        h_ref[3, k] = change
        for c in range(3):
            h_ref[c, k] = terms[c]
            u[c].put(k, -terms[c] * change)

    for k in range(18):
        for c, value in enumerate(jacobi(u, k + 1, [h_ref[c, k + 1] for c in range(4)])):
            v[c].put(k, weighed(value, k - 1))
    for x in range(WX):
        for c, value in enumerate(jacobi(v, x + 1, [h_ref[c, x + 2] for c in range(4)])):
            inner[c, x] = value


def strip_kernel(inner, part, edge_taps, from_left, from_right, out, p_ref, q_ref, s_ref, c_ref, h_ref, u_ref, v_ref):
    x_low, x_high, y_low, y_high = inside()
    lane = iota((1, WY), 1)
    column = strip_column(lane)
    weight = (
        jnp.where(lane < 32, x_low, 1.0)
        * jnp.where(lane >= 96, x_high, 1.0)
        * jnp.where(column < 0, y_low, 1.0)
        * jnp.where(column >= WY, y_high, 1.0)
    )
    p, q, s = Planes(p_ref), Planes(q_ref), Planes(s_ref)
    u, v = [Planes(u_ref, c) for c in range(3)], [Planes(v_ref, c) for c in range(3)]
    for planes, first in [(p, 2), (q, 2), (s, 1)] + [(planes, 1) for planes in u + v]:
        planes.clear(first, first + 7)

    def put(planes, i, value, rim):
        planes.put(i + rim, value)
        if i < rim:
            planes.put(i + rim + 8, pltpu.roll(value, 96, 1))
        if i >= 8 - rim:
            planes.put(i + rim - 8, pltpu.roll(value, 32, 1))

    edges = jnp.concatenate([from_left[...], from_right[...]], axis=1)
    for z_half in range(2):
        found = [part[frame, z_half] + dot(edges, edge_taps[2 * frame + z_half]) for frame in range(2)]
        total, change = (found[0] + found[1]) * 0.25, found[1] - found[0]
        for i in range(16):
            p.put_z(2, 16 * z_half + i, total[8 * i : 8 * i + 8])
            q.put_z(2, 16 * z_half + i, change[8 * i : 8 * i + 8])
    for i in range(8):
        put(p, i, smooth_z(p, i + 2), 2)
        put(q, i, smooth_z(q, i + 2), 2)
    for i in range(8):
        put(s, i, smooth_x(p, i + 2) * weight, 1)
        c_ref[i] = smooth_x(q, i + 2) * weight
    for i in range(8):
        terms, change = gradient_terms(s, i + 1, c_ref[i])
        h_ref[3, i] = change
        for c in range(3):
            h_ref[c, i] = terms[c]
            put(u[c], i, -terms[c] * change, 1)
    for i in range(8):
        for c, value in enumerate(jacobi(u, i + 1, [h_ref[c, i] for c in range(4)])):
            put(v[c], i, value * weight, 1)
    own_lane = iota((NZ, WY), 1)
    rim = (own_lane < 5) | (own_lane >= WY - 5)
    for i in range(8):
        for c, value in enumerate(jacobi(v, i + 1, [h_ref[c, i] for c in range(4)])):
            value = jnp.where((own_lane & 31) < 5, pltpu.roll(value, WY - 22, 1), value)
            for half in range(2):
                x = 8 * half + i
                placed = pltpu.roll(value, WY - 32 * (half + 1) - 5, 1)
                out[c, pl.ds(x, NZ, stride=WX), :] = jnp.where(rim, placed, inner[c, x])


def call(kernel, outs, args, scratch, megabytes, flops):
    moved = sum(a.size * a.dtype.itemsize for a in (*args, *outs))
    spec = pl.BlockSpec(memory_space=pltpu.VMEM)
    return pl.pallas_call(
        kernel,
        out_shape=outs,
        in_specs=[spec] * len(args),
        out_specs=tuple([spec] * len(outs)),
        scratch_shapes=scratch,
        compiler_params=pltpu.CompilerParams(vmem_limit_bytes=megabytes << 20),
        cost_estimate=pl.CostEstimate(flops=flops, bytes_accessed=moved, transcendentals=0),
    )(*args)


def shape(*dims, dtype=F32):
    return jax.ShapeDtypeStruct(dims, dtype)


def on_device(frames, trailing):
    own = frames[0]

    def passed(value, axis, step):
        count = lax.axis_size(axis)
        pairs = [(i, i + step) for i in range(count) if 0 <= i + step < count]
        return lax.ppermute(value, axis, pairs)

    def swapped(value, axis, first):
        pairs = [(i, i + 1) for i in range(first, lax.axis_size(axis) - 1, 2)]
        return lax.ppermute(value, axis, pairs + [(b, a) for a, b in pairs])

    arriving = passed(own, "ta", -1)
    nxt = jnp.where(lax.axis_index("ta") == lax.axis_size("ta") - 1, trailing, arriving)
    upper, lower = jnp.stack([own[:, WX - EDGE :], nxt[:, WX - EDGE :]]), jnp.stack([own[:, :EDGE], nxt[:, :EDGE]])
    even = lax.axis_index("gx") % 2 == 0
    on_chip = swapped(jnp.where(even, upper, lower), "gx", 0)
    off_chip = swapped(jnp.where(even, lower, upper), "gx", 1)
    low, high = jnp.where(even, off_chip, on_chip), jnp.where(even, on_chip, off_chip)
    (packed,) = call(pack_own_kernel, (shape(128, 256, dtype=BF16),), (own, nxt), [], 8, 10**8)
    message = shape(128, 128, dtype=BF16)
    to_right, to_left = call(pack_rim_kernel, (message, message), (low, high, packed), [], 8, 10**8)
    from_left = passed(to_right, "gy", 1)
    from_right = passed(to_left, "gy", -1)
    inner, part, edge_taps = call(
        inner_kernel,
        (shape(3, WX, NZ, WY), shape(2, 2, 128, WY), shape(4, 256, WY, dtype=BF16)),
        (own, nxt, low, high),
        [
            planes_of(32),
            planes_of(32),
            planes_of(22),
            pltpu.VMEM((20, NZ, WY), F32),
            pltpu.VMEM((4, 20, NZ, WY), F32),
            planes_of_3(20),
            planes_of_3(18),
        ],
        16,
        10**9,
    )
    (flow,) = call(
        strip_kernel,
        (shape(3, NZ * WX, WY),),
        (inner, part, edge_taps, from_left, from_right),
        [
            planes_of(12),
            planes_of(12),
            planes_of(10),
            pltpu.VMEM((8, NZ, WY), F32),
            pltpu.VMEM((4, 8, NZ, WY), F32),
            planes_of_3(10),
            planes_of_3(10),
        ],
        16,
        10**8,
    )
    return flow.reshape(1, 3, NZ, WX, WY)


def solution(mesh):
    return jax.shard_map(
        on_device,
        mesh=mesh,
        in_specs=(P("ta", None, "gx", "gy"), P(None, "gx", "gy")),
        out_specs=P("ta", None, None, "gx", "gy"),
        check_vma=False,
    )
```

```python
import jax
import jax.numpy as jnp
from jax import lax
from jax.experimental import pallas as pl
from jax.experimental.pallas import tpu as pltpu
from jax.sharding import PartitionSpec as P

NZ = 32
WX = 16
WY = 128
EDGE = 8
PITCH = 40
F32, BF16 = jnp.float32, jnp.bfloat16


def iota(shape, dim):
    return lax.broadcasted_iota(jnp.int32, shape, dim)


def dot(a, b):
    return jnp.dot(a, b, preferred_element_type=F32)


def y_taps(distance):
    d = jnp.abs(distance)
    tap = jnp.where(d == 0, 6.0, jnp.where(d == 1, 4.0, jnp.where(d == 2, 1.0, 0.0)))
    return tap * (1.0 / 4096.0)


def octet_rows(source, z_half):
    return source[16 * z_half : 16 * z_half + 16].astype(F32).reshape(128, WY).astype(BF16)


def strip_column(lane):
    place = lane & 31
    return jnp.where(place < 16, place - 5, place + 101)


def edge_columns(blocks):
    row, lane = iota((WY, 256), 0), iota((WY, 256), 1)
    column = (lane & 7) + jnp.where(lane < 128, WY - EDGE, 0)
    pick = jnp.where(row == column, 1.0, 0.0).astype(BF16)
    group = (iota((128, 256), 1) & 127) >> 3
    packed = jnp.zeros((128, 256), F32)
    for (octet, frame), block in blocks.items():
        for z_half in range(2):
            found = dot(octet_rows(block, z_half), pick)
            packed = jnp.where(group == (octet * 2 + frame) * 2 + z_half, found, packed)
    return packed.astype(BF16)


def pack_own_kernel(own, nxt, packed):
    packed[...] = edge_columns(
        {
            (octet, frame): block[:, 8 * octet - 8 : 8 * octet, :]
            for octet in (1, 2)
            for frame, block in enumerate((own, nxt))
        }
    )


def pack_rim_kernel(low, high, packed, to_right, to_left):
    rim = edge_columns(
        {(octet, frame): block[frame] for octet, block in ((0, low), (3, high)) for frame in range(2)}
    )
    both = packed[...] + rim
    to_right[...] = both[:, :128]
    to_left[...] = both[:, 128:]


class Planes:
    def __init__(self, ref, index=None):
        self.ref, self.index = ref, index

    def rows(self, start, count, stride=None):
        rows = pl.ds(start, count) if stride is None else pl.ds(start, count, stride=stride)
        return (rows, slice(None)) if self.index is None else (self.index, rows, slice(None))

    def get(self, plane, shift=0):
        return self.ref[self.rows(8 + PITCH * plane + shift, NZ)]

    def put(self, plane, value):
        self.ref[self.rows(8 + PITCH * plane, NZ)] = value

    def put_z(self, plane, z, values):
        self.ref[self.rows(8 + PITCH * plane + z, values.shape[0], PITCH)] = values

    def clear(self, first, last):
        for plane in range(first, last + 2):
            self.ref[self.rows(PITCH * plane, 8)] = jnp.zeros((8, WY), F32)


def planes_of(count):
    return pltpu.VMEM((8 + PITCH * count, WY), F32)


def planes_of_3(count):
    return pltpu.VMEM((3, 8 + PITCH * count, WY), F32)


def smooth_z(planes, k):
    near = planes.get(k, 1) + planes.get(k, -1)
    far = planes.get(k, 2) + planes.get(k, -2)
    return 6.0 * planes.get(k) + 4.0 * near + far


def smooth_x(planes, k):
    near = planes.get(k + 1) + planes.get(k - 1)
    far = planes.get(k + 2) + planes.get(k - 2)
    return 6.0 * planes.get(k) + 4.0 * near + far


def y_pair(v):
    return pltpu.roll(v, WY - 1, 1), pltpu.roll(v, 1, 1)


def gradient_terms(s, k, change):
    y_next, y_prev = y_pair(s.get(k))
    grads = (s.get(k + 1) - s.get(k - 1), y_next - y_prev, s.get(k, 1) - s.get(k, -1))
    denom = 0.01 + grads[0] * grads[0] + grads[1] * grads[1] + grads[2] * grads[2]
    scale = lax.rsqrt(denom)
    scale = scale * (1.5 - 0.5 * denom * scale * scale)
    return [grad * scale for grad in grads], change * scale


def jacobi(velocity, k, terms):
    means = []
    for planes in velocity:
        y_next, y_prev = y_pair(planes.get(k))
        total = (planes.get(k + 1) + planes.get(k - 1)) + (y_next + y_prev)
        total = total + (planes.get(k, 1) + planes.get(k, -1))
        means.append(total * (1.0 / 6.0))
    common = terms[3] + terms[0] * means[0] + terms[1] * means[1] + terms[2] * means[2]
    return [mean - term * common for mean, term in zip(means, terms)]


def inside():
    faces = []
    for axis in ("gx", "gy"):
        at = lax.axis_index(axis)
        faces += [jnp.where(at == 0, 0.0, 1.0), jnp.where(at == lax.axis_size(axis) - 1, 0.0, 1.0)]
    return faces


def inner_kernel(own, nxt, low, high, inner, part, edge_taps, p_ref, q_ref, s_ref, c_ref, h_ref, u_ref, v_ref):
    x_low, x_high, _, _ = inside()

    def weight(x):
        return x_low if x < 0 else x_high if x >= WX else None

    def weighed(value, x):
        return value if weight(x) is None else value * weight(x)

    p, q, s = Planes(p_ref), Planes(q_ref), Planes(s_ref)
    u, v = [Planes(u_ref, c) for c in range(3)], [Planes(v_ref, c) for c in range(3)]
    p.clear(3, 28)
    q.clear(3, 28)
    s.clear(1, 20)
    for c in range(3):
        u[c].clear(1, 18)
        v[c].clear(1, 16)

    row, lane = iota((WY, WY), 0), iota((WY, WY), 1)
    taps = y_taps(lane - row).astype(BF16)
    strip_taps = y_taps(strip_column(lane) - row)
    octet_taps = jnp.concatenate(
        [jnp.where((lane >> 5) == octet, strip_taps, 0.0) for octet in range(4)], axis=0
    ).astype(BF16)

    row, lane = iota((256, WY), 0), iota((256, WY), 1)
    column = (row & 7) + jnp.where(row < 128, -EDGE, WY)
    edge = jnp.where(((row & 127) >> 5) == (lane >> 5), y_taps(strip_column(lane) - column), 0.0)
    for group in range(4):
        edge_taps[group] = jnp.where(((row >> 3) & 3) == group, edge, 0.0).astype(BF16)

    for z_half in range(2):
        octets = [[], []]
        for octet in range(4):
            found = []
            for frame, centre in enumerate((own, nxt)):
                block = (
                    (low if octet == 0 else high)[frame, 16 * z_half : 16 * z_half + 16]
                    if octet in (0, 3)
                    else centre[16 * z_half : 16 * z_half + 16, 8 * octet - 8 : 8 * octet, :]
                )
                rows = block.astype(F32).reshape(128, WY).astype(BF16)
                octets[frame].append(rows)
                found.append(dot(rows, taps))
            total, change = (found[0] + found[1]) * 0.25, found[1] - found[0]
            for i in range(16):
                p.put_z(8 * octet, 16 * z_half + i, total[8 * i : 8 * i + 8])
                q.put_z(8 * octet, 16 * z_half + i, change[8 * i : 8 * i + 8])
        for frame in range(2):
            part[frame, z_half] = dot(jnp.concatenate(octets[frame], axis=1), octet_taps)

    for k in range(3, 29):
        p.put(k, smooth_z(p, k))
        q.put(k, smooth_z(q, k))
    for k in range(22):
        s.put(k, weighed(smooth_x(p, k + 5), k - 3))
        if 1 <= k <= 20:
            c_ref[k - 1] = weighed(smooth_x(q, k + 5), k - 3)

    for k in range(20):
        terms, change = gradient_terms(s, k + 1, c_ref[k])
        h_ref[3, k] = change
        for c in range(3):
            h_ref[c, k] = terms[c]
            u[c].put(k, -terms[c] * change)

    for k in range(18):
        for c, value in enumerate(jacobi(u, k + 1, [h_ref[c, k + 1] for c in range(4)])):
            v[c].put(k, weighed(value, k - 1))
    for x in range(WX):
        for c, value in enumerate(jacobi(v, x + 1, [h_ref[c, x + 2] for c in range(4)])):
            inner[c, x] = value


def strip_kernel(inner, part, edge_taps, from_left, from_right, out, p_ref, q_ref, s_ref, c_ref, h_ref, u_ref, v_ref, w_ref, done_ref, sems):
    x_low, x_high, y_low, y_high = inside()
    lane = iota((1, WY), 1)
    column = strip_column(lane)
    weight = (
        jnp.where(lane < 32, x_low, 1.0)
        * jnp.where(lane >= 96, x_high, 1.0)
        * jnp.where(column < 0, y_low, 1.0)
        * jnp.where(column >= WY, y_high, 1.0)
    )
    p, q, s = Planes(p_ref), Planes(q_ref), Planes(s_ref)
    u, v = [Planes(u_ref, c) for c in range(3)], [Planes(v_ref, c) for c in range(3)]
    for planes, first in [(p, 2), (q, 2), (s, 1)] + [(planes, 1) for planes in u + v]:
        planes.clear(first, first + 7)

    def put(planes, i, value, rim):
        planes.put(i + rim, value)
        if i < rim:
            planes.put(i + rim + 8, pltpu.roll(value, 96, 1))
        if i >= 8 - rim:
            planes.put(i + rim - 8, pltpu.roll(value, 32, 1))

    edges = jnp.concatenate([from_left[...], from_right[...]], axis=1)
    for z_half in range(2):
        found = [part[frame, z_half] + dot(edges, edge_taps[2 * frame + z_half]) for frame in range(2)]
        total, change = (found[0] + found[1]) * 0.25, found[1] - found[0]
        for i in range(16):
            p.put_z(2, 16 * z_half + i, total[8 * i : 8 * i + 8])
            q.put_z(2, 16 * z_half + i, change[8 * i : 8 * i + 8])
    for i in range(8):
        put(p, i, smooth_z(p, i + 2), 2)
        put(q, i, smooth_z(q, i + 2), 2)
    for i in range(8):
        put(s, i, smooth_x(p, i + 2) * weight, 1)
        c_ref[i] = smooth_x(q, i + 2) * weight
    for i in range(8):
        terms, change = gradient_terms(s, i + 1, c_ref[i])
        h_ref[3, i] = change
        for c in range(3):
            h_ref[c, i] = terms[c]
            put(u[c], i, -terms[c] * change, 1)
    for i in range(8):
        for c, value in enumerate(jacobi(u, i + 1, [h_ref[c, i] for c in range(4)])):
            put(v[c], i, value * weight, 1)
    for i in range(8):
        for c, value in enumerate(jacobi(v, i + 1, [h_ref[c, i] for c in range(4)])):
            w_ref[c, NZ * i : NZ * i + NZ, :] = value
    row, lane = iota((WY, 256), 0), iota((WY, 256), 1)
    place, to = row & 31, lane & 127
    pick = ((row >> 5) - 1 == (lane >> 7)) & ((to == place - 5) | (to == place + 101))
    pick = jnp.where(pick, 1.0, 0.0).astype(BF16)
    own_lane = iota((NZ, WY), 1)
    rim = (own_lane < 5) | (own_lane >= WY - 5)
    for c in range(3):
        rest = w_ref[c]
        placed = jnp.zeros((8 * NZ, 256), F32)
        for _ in range(3):
            term = rest.astype(BF16)
            rest = rest - term.astype(F32)
            placed = placed + dot(term, pick)
        for i in range(8):
            for half in range(2):
                x = 8 * half + i
                found = placed[NZ * i : NZ * i + NZ, 128 * half : 128 * half + 128]
                done_ref[c, pl.ds(x, NZ, stride=WX), :] = jnp.where(rim, found, inner[c, x])
        pltpu.make_async_copy(done_ref.at[c], out.at[c], sems.at[c]).start()
    for c in range(3):
        pltpu.make_async_copy(done_ref.at[c], out.at[c], sems.at[c]).wait()


def call(kernel, outs, args, scratch, megabytes, flops, out_space=pltpu.VMEM):
    moved = sum(a.size * a.dtype.itemsize for a in (*args, *outs))
    spec = pl.BlockSpec(memory_space=pltpu.VMEM)
    return pl.pallas_call(
        kernel,
        out_shape=outs,
        in_specs=[spec] * len(args),
        out_specs=tuple([pl.BlockSpec(memory_space=out_space)] * len(outs)),
        scratch_shapes=scratch,
        compiler_params=pltpu.CompilerParams(vmem_limit_bytes=megabytes << 20),
        cost_estimate=pl.CostEstimate(flops=flops, bytes_accessed=moved, transcendentals=0),
    )(*args)


def shape(*dims, dtype=F32):
    return jax.ShapeDtypeStruct(dims, dtype)


def on_device(frames, trailing):
    own = frames[0]

    def passed(value, axis, step):
        count = lax.axis_size(axis)
        pairs = [(i, i + step) for i in range(count) if 0 <= i + step < count]
        return lax.ppermute(value, axis, pairs)

    def swapped(value, axis, first):
        pairs = [(i, i + 1) for i in range(first, lax.axis_size(axis) - 1, 2)]
        return lax.ppermute(value, axis, pairs + [(b, a) for a, b in pairs])

    arriving = passed(own, "ta", -1)
    nxt = jnp.where(lax.axis_index("ta") == lax.axis_size("ta") - 1, trailing, arriving)
    upper, lower = jnp.stack([own[:, WX - EDGE :], nxt[:, WX - EDGE :]]), jnp.stack([own[:, :EDGE], nxt[:, :EDGE]])
    even = lax.axis_index("gx") % 2 == 0
    on_chip = swapped(jnp.where(even, upper, lower), "gx", 0)
    off_chip = swapped(jnp.where(even, lower, upper), "gx", 1)
    low, high = jnp.where(even, off_chip, on_chip), jnp.where(even, on_chip, off_chip)
    (packed,) = call(pack_own_kernel, (shape(128, 256, dtype=BF16),), (own, nxt), [], 8, 10**8)
    message = shape(128, 128, dtype=BF16)
    to_right, to_left = call(pack_rim_kernel, (message, message), (low, high, packed), [], 8, 10**8)
    from_left = passed(to_right, "gy", 1)
    from_right = passed(to_left, "gy", -1)
    inner, part, edge_taps = call(
        inner_kernel,
        (shape(3, WX, NZ, WY), shape(2, 2, 128, WY), shape(4, 256, WY, dtype=BF16)),
        (own, nxt, low, high),
        [
            planes_of(32),
            planes_of(32),
            planes_of(22),
            pltpu.VMEM((20, NZ, WY), F32),
            pltpu.VMEM((4, 20, NZ, WY), F32),
            planes_of_3(20),
            planes_of_3(18),
        ],
        16,
        10**9,
    )
    (flow,) = call(
        strip_kernel,
        (shape(3, NZ * WX, WY),),
        (inner, part, edge_taps, from_left, from_right),
        [
            planes_of(12),
            planes_of(12),
            planes_of(10),
            pltpu.VMEM((8, NZ, WY), F32),
            pltpu.VMEM((4, 8, NZ, WY), F32),
            planes_of_3(10),
            planes_of_3(10),
            pltpu.VMEM((3, 8 * NZ, WY), F32),
            pltpu.VMEM((3, NZ * WX, WY), F32),
            pltpu.SemaphoreType.DMA((3,)),
        ],
        16,
        10**8,
        pl.ANY,
    )
    return flow.reshape(1, 3, NZ, WX, WY)


def solution(mesh):
    return jax.shard_map(
        on_device,
        mesh=mesh,
        in_specs=(P("ta", None, "gx", "gy"), P(None, "gx", "gy")),
        out_specs=P("ta", None, None, "gx", "gy"),
        check_vma=False,
    )
```

```python
import jax
import jax.numpy as jnp
from jax import lax
from jax.experimental import pallas as pl
from jax.experimental.pallas import tpu as pltpu
from jax.sharding import PartitionSpec as P

NZ = 32
WX = 16
WY = 128
EDGE = 8
PITCH = 40
F32, BF16 = jnp.float32, jnp.bfloat16


def iota(shape, dim):
    return lax.broadcasted_iota(jnp.int32, shape, dim)


def dot(a, b):
    return jnp.dot(a, b, preferred_element_type=F32)


def y_taps(distance):
    d = jnp.abs(distance)
    tap = jnp.where(d == 0, 6.0, jnp.where(d == 1, 4.0, jnp.where(d == 2, 1.0, 0.0)))
    return tap * (1.0 / 4096.0)


def octet_rows(source, z_half):
    return source[16 * z_half : 16 * z_half + 16].astype(F32).reshape(128, WY).astype(BF16)


def strip_column(lane):
    place = lane & 31
    return jnp.where(place < 16, place - 5, place + 101)


def edge_columns(blocks, pick):
    group = (iota((128, 256), 1) & 127) >> 3
    packed = jnp.zeros((128, 256), F32)
    for (octet, frame), block in blocks.items():
        for z_half in range(2):
            found = dot(octet_rows(block, z_half), pick)
            packed = jnp.where(group == (octet * 2 + frame) * 2 + z_half, found, packed)
    return packed.astype(BF16)


def own_octets(block, frame):
    return {(octet, frame): block[:, 8 * octet - 8 : 8 * octet, :] for octet in (1, 2)}


def front_kernel(own, packed, pick, taps, octet_taps, edge_taps, place):
    row, lane = iota((WY, 256), 0), iota((WY, 256), 1)
    column = (lane & 7) + jnp.where(lane < 128, WY - EDGE, 0)
    pick[...] = jnp.where(row == column, 1.0, 0.0).astype(BF16)
    packed[...] = edge_columns(own_octets(own, 0), pick[...])

    at, to = row & 31, lane & 127
    hit = ((row >> 5) - 1 == (lane >> 7)) & ((to == at - 5) | (to == at + 101))
    place[...] = jnp.where(hit, 1.0, 0.0).astype(BF16)

    row, lane = iota((WY, WY), 0), iota((WY, WY), 1)
    taps[...] = y_taps(lane - row).astype(BF16)
    strip_taps = y_taps(strip_column(lane) - row)
    for octet in range(4):
        octet_taps[WY * octet : WY * octet + WY, :] = jnp.where((lane >> 5) == octet, strip_taps, 0.0).astype(BF16)

    row, lane = iota((256, WY), 0), iota((256, WY), 1)
    column = (row & 7) + jnp.where(row < 128, -EDGE, WY)
    edge = jnp.where(((row & 127) >> 5) == (lane >> 5), y_taps(strip_column(lane) - column), 0.0)
    for group in range(4):
        edge_taps[group] = jnp.where(((row >> 3) & 3) == group, edge, 0.0).astype(BF16)


def pack_kernel(nxt, low, high, packed, pick, to_right, to_left):
    blocks = own_octets(nxt, 1)
    blocks |= {(octet, frame): block[frame] for octet, block in ((0, low), (3, high)) for frame in range(2)}
    both = packed[...] + edge_columns(blocks, pick[...])
    to_right[...] = both[:, :128]
    to_left[...] = both[:, 128:]


class Planes:
    def __init__(self, ref, index=None):
        self.ref, self.index = ref, index

    def rows(self, start, count, stride=None):
        rows = pl.ds(start, count) if stride is None else pl.ds(start, count, stride=stride)
        return (rows, slice(None)) if self.index is None else (self.index, rows, slice(None))

    def get(self, plane, shift=0):
        return self.ref[self.rows(8 + PITCH * plane + shift, NZ)]

    def put(self, plane, value):
        self.ref[self.rows(8 + PITCH * plane, NZ)] = value

    def put_z(self, plane, z, values):
        self.ref[self.rows(8 + PITCH * plane + z, values.shape[0], PITCH)] = values

    def clear(self, first, last):
        for plane in range(first, last + 2):
            self.ref[self.rows(PITCH * plane, 8)] = jnp.zeros((8, WY), F32)


def planes_of(count):
    return pltpu.VMEM((8 + PITCH * count, WY), F32)


def planes_of_3(count):
    return pltpu.VMEM((3, 8 + PITCH * count, WY), F32)


def smooth_z(planes, k):
    near = planes.get(k, 1) + planes.get(k, -1)
    far = planes.get(k, 2) + planes.get(k, -2)
    return 6.0 * planes.get(k) + 4.0 * near + far


def smooth_x(planes, k):
    near = planes.get(k + 1) + planes.get(k - 1)
    far = planes.get(k + 2) + planes.get(k - 2)
    return 6.0 * planes.get(k) + 4.0 * near + far


def y_pair(v):
    return pltpu.roll(v, WY - 1, 1), pltpu.roll(v, 1, 1)


def gradient_terms(s, k, change):
    y_next, y_prev = y_pair(s.get(k))
    grads = (s.get(k + 1) - s.get(k - 1), y_next - y_prev, s.get(k, 1) - s.get(k, -1))
    denom = 0.01 + grads[0] * grads[0] + grads[1] * grads[1] + grads[2] * grads[2]
    scale = lax.rsqrt(denom)
    scale = scale * (1.5 - 0.5 * denom * scale * scale)
    return [grad * scale for grad in grads], change * scale


def jacobi(velocity, k, terms):
    means = []
    for planes in velocity:
        y_next, y_prev = y_pair(planes.get(k))
        total = (planes.get(k + 1) + planes.get(k - 1)) + (y_next + y_prev)
        total = total + (planes.get(k, 1) + planes.get(k, -1))
        means.append(total * (1.0 / 6.0))
    common = terms[3] + terms[0] * means[0] + terms[1] * means[1] + terms[2] * means[2]
    return [mean - term * common for mean, term in zip(means, terms)]


def inside():
    faces = []
    for axis in ("gx", "gy"):
        at = lax.axis_index(axis)
        faces += [jnp.where(at == 0, 0.0, 1.0), jnp.where(at == lax.axis_size(axis) - 1, 0.0, 1.0)]
    return faces


def inner_kernel(own, nxt, low, high, taps, octet_taps, inner, part, p_ref, q_ref, s_ref, c_ref, h_ref, u_ref, v_ref):
    x_low, x_high, _, _ = inside()

    def weight(x):
        return x_low if x < 0 else x_high if x >= WX else None

    def weighed(value, x):
        return value if weight(x) is None else value * weight(x)

    p, q, s = Planes(p_ref), Planes(q_ref), Planes(s_ref)
    u, v = [Planes(u_ref, c) for c in range(3)], [Planes(v_ref, c) for c in range(3)]
    p.clear(3, 28)
    q.clear(3, 28)
    s.clear(1, 20)
    for c in range(3):
        u[c].clear(1, 18)
        v[c].clear(1, 16)

    for z_half in range(2):
        octets = [[], []]
        for octet in range(4):
            found = []
            for frame, centre in enumerate((own, nxt)):
                block = (
                    (low if octet == 0 else high)[frame, 16 * z_half : 16 * z_half + 16]
                    if octet in (0, 3)
                    else centre[16 * z_half : 16 * z_half + 16, 8 * octet - 8 : 8 * octet, :]
                )
                rows = block.astype(F32).reshape(128, WY).astype(BF16)
                octets[frame].append(rows)
                found.append(dot(rows, taps[...]))
            total, change = (found[0] + found[1]) * 0.25, found[1] - found[0]
            for i in range(16):
                p.put_z(8 * octet, 16 * z_half + i, total[8 * i : 8 * i + 8])
                q.put_z(8 * octet, 16 * z_half + i, change[8 * i : 8 * i + 8])
        for frame in range(2):
            part[frame, z_half] = dot(jnp.concatenate(octets[frame], axis=1), octet_taps[...])

    for k in range(3, 29):
        p.put(k, smooth_z(p, k))
        q.put(k, smooth_z(q, k))
    for k in range(22):
        s.put(k, weighed(smooth_x(p, k + 5), k - 3))
        if 1 <= k <= 20:
            c_ref[k - 1] = weighed(smooth_x(q, k + 5), k - 3)

    for k in range(20):
        terms, change = gradient_terms(s, k + 1, c_ref[k])
        h_ref[3, k] = change
        for c in range(3):
            h_ref[c, k] = terms[c]
            u[c].put(k, -terms[c] * change)

    for k in range(18):
        for c, value in enumerate(jacobi(u, k + 1, [h_ref[c, k + 1] for c in range(4)])):
            v[c].put(k, weighed(value, k - 1))
    for x in range(WX):
        for c, value in enumerate(jacobi(v, x + 1, [h_ref[c, x + 2] for c in range(4)])):
            inner[c, x] = value


def strip_kernel(inner, part, edge_taps, place, from_left, from_right, out, p_ref, q_ref, s_ref, c_ref, h_ref, u_ref, v_ref, w_ref, done_ref, sems):
    x_low, x_high, y_low, y_high = inside()
    lane = iota((1, WY), 1)
    column = strip_column(lane)
    weight = (
        jnp.where(lane < 32, x_low, 1.0)
        * jnp.where(lane >= 96, x_high, 1.0)
        * jnp.where(column < 0, y_low, 1.0)
        * jnp.where(column >= WY, y_high, 1.0)
    )
    p, q, s = Planes(p_ref), Planes(q_ref), Planes(s_ref)
    u, v = [Planes(u_ref, c) for c in range(3)], [Planes(v_ref, c) for c in range(3)]
    for planes, first in [(p, 2), (q, 2), (s, 1)] + [(planes, 1) for planes in u + v]:
        planes.clear(first, first + 7)

    def put(planes, i, value, rim):
        planes.put(i + rim, value)
        if i < rim:
            planes.put(i + rim + 8, pltpu.roll(value, 96, 1))
        if i >= 8 - rim:
            planes.put(i + rim - 8, pltpu.roll(value, 32, 1))

    edges = jnp.concatenate([from_left[...], from_right[...]], axis=1)
    for z_half in range(2):
        found = [part[frame, z_half] + dot(edges, edge_taps[2 * frame + z_half]) for frame in range(2)]
        total, change = (found[0] + found[1]) * 0.25, found[1] - found[0]
        for i in range(16):
            p.put_z(2, 16 * z_half + i, total[8 * i : 8 * i + 8])
            q.put_z(2, 16 * z_half + i, change[8 * i : 8 * i + 8])
    for i in range(8):
        put(p, i, smooth_z(p, i + 2), 2)
        put(q, i, smooth_z(q, i + 2), 2)
    for i in range(8):
        put(s, i, smooth_x(p, i + 2) * weight, 1)
        c_ref[i] = smooth_x(q, i + 2) * weight
    for i in range(8):
        terms, change = gradient_terms(s, i + 1, c_ref[i])
        h_ref[3, i] = change
        for c in range(3):
            h_ref[c, i] = terms[c]
            put(u[c], i, -terms[c] * change, 1)
    for i in range(8):
        for c, value in enumerate(jacobi(u, i + 1, [h_ref[c, i] for c in range(4)])):
            put(v[c], i, value * weight, 1)
    for i in range(8):
        for c, value in enumerate(jacobi(v, i + 1, [h_ref[c, i] for c in range(4)])):
            w_ref[c, NZ * i : NZ * i + NZ, :] = value
    own_lane = iota((NZ, WY), 1)
    rim = (own_lane < 5) | (own_lane >= WY - 5)
    for c in range(3):
        rest = w_ref[c]
        placed = jnp.zeros((8 * NZ, 256), F32)
        for _ in range(3):
            term = rest.astype(BF16)
            rest = rest - term.astype(F32)
            placed = placed + dot(term, place[...])
        for i in range(8):
            for half in range(2):
                x = 8 * half + i
                found = placed[NZ * i : NZ * i + NZ, 128 * half : 128 * half + 128]
                done_ref[c, pl.ds(x, NZ, stride=WX), :] = jnp.where(rim, found, inner[c, x])
        pltpu.make_async_copy(done_ref.at[c], out.at[c], sems.at[c]).start()
    for c in range(3):
        pltpu.make_async_copy(done_ref.at[c], out.at[c], sems.at[c]).wait()


def call(kernel, outs, args, scratch, megabytes, flops, out_space=pltpu.VMEM):
    moved = sum(a.size * a.dtype.itemsize for a in (*args, *outs))
    spec = pl.BlockSpec(memory_space=pltpu.VMEM)
    return pl.pallas_call(
        kernel,
        out_shape=outs,
        in_specs=[spec] * len(args),
        out_specs=tuple([pl.BlockSpec(memory_space=out_space)] * len(outs)),
        scratch_shapes=scratch,
        compiler_params=pltpu.CompilerParams(vmem_limit_bytes=megabytes << 20),
        cost_estimate=pl.CostEstimate(flops=flops, bytes_accessed=moved, transcendentals=0),
    )(*args)


def shape(*dims, dtype=F32):
    return jax.ShapeDtypeStruct(dims, dtype)


def on_device(frames, trailing):
    own = frames[0]

    def passed(value, axis, step):
        count = lax.axis_size(axis)
        pairs = [(i, i + step) for i in range(count) if 0 <= i + step < count]
        return lax.ppermute(value, axis, pairs)

    def swapped(value, axis, first):
        pairs = [(i, i + 1) for i in range(first, lax.axis_size(axis) - 1, 2)]
        return lax.ppermute(value, axis, pairs + [(b, a) for a, b in pairs])

    arriving = passed(own, "ta", -1)
    packed, pick, taps, octet_taps, edge_taps, place = call(
        front_kernel,
        tuple(
            shape(*dims, dtype=BF16)
            for dims in ((128, 256), (WY, 256), (WY, WY), (4 * WY, WY), (4, 256, WY), (WY, 256))
        ),
        (own,),
        [],
        8,
        10**8,
    )
    nxt = jnp.where(lax.axis_index("ta") == lax.axis_size("ta") - 1, trailing, arriving)
    upper, lower = jnp.stack([own[:, WX - EDGE :], nxt[:, WX - EDGE :]]), jnp.stack([own[:, :EDGE], nxt[:, :EDGE]])
    even = lax.axis_index("gx") % 2 == 0
    off_chip = swapped(jnp.where(even, lower, upper), "gx", 1)
    pairs = [[i, i + 1] for i in range(0, lax.axis_size("gx"), 2)]
    both = lax.all_gather(jnp.where(even, upper, lower), "gx", axis_index_groups=pairs)
    on_chip = jnp.where(even, both[1], both[0])
    low, high = jnp.where(even, off_chip, on_chip), jnp.where(even, on_chip, off_chip)
    message = shape(128, 128, dtype=BF16)
    to_right, to_left = call(pack_kernel, (message, message), (nxt, low, high, packed, pick), [], 8, 10**8)
    from_left = passed(to_right, "gy", 1)
    from_right = passed(to_left, "gy", -1)
    inner, part = call(
        inner_kernel,
        (shape(3, WX, NZ, WY), shape(2, 2, 128, WY)),
        (own, nxt, low, high, taps, octet_taps),
        [
            planes_of(32),
            planes_of(32),
            planes_of(22),
            pltpu.VMEM((20, NZ, WY), F32),
            pltpu.VMEM((4, 20, NZ, WY), F32),
            planes_of_3(20),
            planes_of_3(18),
        ],
        16,
        10**9,
    )
    (flow,) = call(
        strip_kernel,
        (shape(3, NZ * WX, WY),),
        (inner, part, edge_taps, place, from_left, from_right),
        [
            planes_of(12),
            planes_of(12),
            planes_of(10),
            pltpu.VMEM((8, NZ, WY), F32),
            pltpu.VMEM((4, 8, NZ, WY), F32),
            planes_of_3(10),
            planes_of_3(10),
            pltpu.VMEM((3, 8 * NZ, WY), F32),
            pltpu.VMEM((3, NZ * WX, WY), F32),
            pltpu.SemaphoreType.DMA((3,)),
        ],
        16,
        10**8,
        pl.ANY,
    )
    return flow.reshape(1, 3, NZ, WX, WY)


def solution(mesh):
    return jax.shard_map(
        on_device,
        mesh=mesh,
        in_specs=(P("ta", None, "gx", "gy"), P(None, "gx", "gy")),
        out_specs=P("ta", None, None, "gx", "gy"),
        check_vma=False,
    )
```

```python
import jax
import jax.numpy as jnp
from jax import lax
from jax.experimental import pallas as pl
from jax.experimental.pallas import tpu as pltpu
from jax.sharding import PartitionSpec as P

NZ = 32
WX = 16
WY = 128
EDGE = 8
PITCH = 40
F32, BF16 = jnp.float32, jnp.bfloat16


def iota(shape, dim):
    return lax.broadcasted_iota(jnp.int32, shape, dim)


def dot(a, b):
    return jnp.dot(a, b, preferred_element_type=F32)


def y_taps(distance):
    d = jnp.abs(distance)
    tap = jnp.where(d == 0, 6.0, jnp.where(d == 1, 4.0, jnp.where(d == 2, 1.0, 0.0)))
    return tap * (1.0 / 4096.0)


def octet_rows(source, z_half):
    return source[16 * z_half : 16 * z_half + 16].astype(F32).reshape(128, WY).astype(BF16)


def strip_column(lane):
    place = lane & 31
    return jnp.where(place < 16, place - 5, place + 101)


def edge_columns(blocks, pick):
    group = (iota((128, 256), 1) & 127) >> 3
    packed = jnp.zeros((128, 256), F32)
    for (octet, frame), block in blocks.items():
        for z_half in range(2):
            found = dot(octet_rows(block, z_half), pick)
            packed = jnp.where(group == (octet * 2 + frame) * 2 + z_half, found, packed)
    return packed.astype(BF16)


def own_octets(block, frame):
    return {(octet, frame): block[:, 8 * octet - 8 : 8 * octet, :] for octet in (1, 2)}


def front_kernel(
    own, low, high, packed, pick, taps, octet_taps, edge_taps, place, smooth, part, p_ref
):
    row, lane = iota((WY, 256), 0), iota((WY, 256), 1)
    column = (lane & 7) + jnp.where(lane < 128, WY - EDGE, 0)
    pick[...] = jnp.where(row == column, 1.0, 0.0).astype(BF16)
    packed[...] = edge_columns(own_octets(own, 0) | {(0, 0): low, (3, 0): high}, pick[...])

    at, to = row & 31, lane & 127
    hit = ((row >> 5) - 1 == (lane >> 7)) & ((to == at - 5) | (to == at + 101))
    place[...] = jnp.where(hit, 1.0, 0.0).astype(BF16)

    row, lane = iota((WY, WY), 0), iota((WY, WY), 1)
    taps[...] = y_taps(lane - row).astype(BF16)
    strip_taps = y_taps(strip_column(lane) - row)
    for octet in range(4):
        octet_taps[WY * octet : WY * octet + WY, :] = jnp.where((lane >> 5) == octet, strip_taps, 0.0).astype(BF16)

    row, lane = iota((256, WY), 0), iota((256, WY), 1)
    column = (row & 7) + jnp.where(row < 128, -EDGE, WY)
    edge = jnp.where(((row & 127) >> 5) == (lane >> 5), y_taps(strip_column(lane) - column), 0.0)
    for group in range(4):
        edge_taps[group] = jnp.where(((row >> 3) & 3) == group, edge, 0.0).astype(BF16)

    p = Planes(p_ref)
    smooth_yz(p, own, low, high, taps, octet_taps, part)
    for k in range(22):
        smooth[k] = smooth_x(p, k + 5)


def pack_kernel(nxt, low, high, packed, pick, to_right, to_left):
    both = packed[...] + edge_columns(own_octets(nxt, 1) | {(0, 1): low, (3, 1): high}, pick[...])
    to_right[...] = both[:, :128]
    to_left[...] = both[:, 128:]


class Planes:
    def __init__(self, ref, index=None):
        self.ref, self.index = ref, index

    def rows(self, start, count, stride=None):
        rows = pl.ds(start, count) if stride is None else pl.ds(start, count, stride=stride)
        return (rows, slice(None)) if self.index is None else (self.index, rows, slice(None))

    def get(self, plane, shift=0):
        return self.ref[self.rows(8 + PITCH * plane + shift, NZ)]

    def put(self, plane, value):
        self.ref[self.rows(8 + PITCH * plane, NZ)] = value

    def put_z(self, plane, z, values):
        self.ref[self.rows(8 + PITCH * plane + z, values.shape[0], PITCH)] = values

    def clear(self, first, last):
        for plane in range(first, last + 2):
            self.ref[self.rows(PITCH * plane, 8)] = jnp.zeros((8, WY), F32)


def planes_of(count):
    return pltpu.VMEM((8 + PITCH * count, WY), F32)


def planes_of_3(count):
    return pltpu.VMEM((3, 8 + PITCH * count, WY), F32)


def smooth_z(planes, k):
    near = planes.get(k, 1) + planes.get(k, -1)
    far = planes.get(k, 2) + planes.get(k, -2)
    return 6.0 * planes.get(k) + 4.0 * near + far


def smooth_x(planes, k):
    near = planes.get(k + 1) + planes.get(k - 1)
    far = planes.get(k + 2) + planes.get(k - 2)
    return 6.0 * planes.get(k) + 4.0 * near + far


def y_pair(v):
    return pltpu.roll(v, WY - 1, 1), pltpu.roll(v, 1, 1)


def gradient_terms(s, k, change):
    y_next, y_prev = y_pair(s.get(k))
    grads = (s.get(k + 1) - s.get(k - 1), y_next - y_prev, s.get(k, 1) - s.get(k, -1))
    denom = 0.01 + grads[0] * grads[0] + grads[1] * grads[1] + grads[2] * grads[2]
    scale = lax.rsqrt(denom)
    scale = scale * (1.5 - 0.5 * denom * scale * scale)
    return [grad * scale for grad in grads], change * scale


def jacobi(velocity, k, terms):
    means = []
    for planes in velocity:
        y_next, y_prev = y_pair(planes.get(k))
        total = (planes.get(k + 1) + planes.get(k - 1)) + (y_next + y_prev)
        total = total + (planes.get(k, 1) + planes.get(k, -1))
        means.append(total * (1.0 / 6.0))
    common = terms[3] + terms[0] * means[0] + terms[1] * means[1] + terms[2] * means[2]
    return [mean - term * common for mean, term in zip(means, terms)]


def smooth_yz(p, frame, low, high, taps, octet_taps, part):
    p.clear(3, 28)
    for z_half in range(2):
        zs = slice(16 * z_half, 16 * z_half + 16)
        octets = []
        for octet in range(4):
            block = (
                frame[zs, 8 * octet - 8 : 8 * octet, :] if octet in (1, 2) else (low if octet == 0 else high)[zs]
            )
            rows = block.astype(F32).reshape(128, WY).astype(BF16)
            octets.append(rows)
            found = dot(rows, taps[...])
            for i in range(16):
                p.put_z(8 * octet, 16 * z_half + i, found[8 * i : 8 * i + 8])
        part[z_half] = dot(jnp.concatenate(octets, axis=1), octet_taps[...])
    for k in range(3, 29):
        p.put(k, smooth_z(p, k))


def inside():
    faces = []
    for axis in ("gx", "gy"):
        at = lax.axis_index(axis)
        faces += [jnp.where(at == 0, 0.0, 1.0), jnp.where(at == lax.axis_size(axis) - 1, 0.0, 1.0)]
    return faces


def inner_kernel(
    nxt, low, high, taps, octet_taps, smooth, inner, part, p_ref, s_ref, c_ref, h_ref, u_ref, v_ref
):
    x_low, x_high, _, _ = inside()

    def weight(x):
        return x_low if x < 0 else x_high if x >= WX else None

    def weighed(value, x):
        return value if weight(x) is None else value * weight(x)

    p, s = Planes(p_ref), Planes(s_ref)
    u, v = [Planes(u_ref, c) for c in range(3)], [Planes(v_ref, c) for c in range(3)]
    s.clear(1, 20)
    for c in range(3):
        u[c].clear(1, 18)
        v[c].clear(1, 16)
    smooth_yz(p, nxt, low, high, taps, octet_taps, part)

    for k in range(22):
        first, second = smooth[k], smooth_x(p, k + 5)
        s.put(k, weighed((first + second) * 0.25, k - 3))
        if 1 <= k <= 20:
            c_ref[k - 1] = weighed(second - first, k - 3)

    for k in range(20):
        terms, change = gradient_terms(s, k + 1, c_ref[k])
        h_ref[3, k] = change
        for c in range(3):
            h_ref[c, k] = terms[c]
            u[c].put(k, -terms[c] * change)

    for k in range(18):
        for c, value in enumerate(jacobi(u, k + 1, [h_ref[c, k + 1] for c in range(4)])):
            v[c].put(k, weighed(value, k - 1))
    for x in range(WX):
        for c, value in enumerate(jacobi(v, x + 1, [h_ref[c, x + 2] for c in range(4)])):
            inner[c, x] = value


def strip_kernel(
    inner, part_own, part_nxt, edge_taps, place, from_left, from_right, out,
    p_ref, q_ref, s_ref, c_ref, h_ref, u_ref, v_ref, w_ref, done_ref, sems,
):
    x_low, x_high, y_low, y_high = inside()
    lane = iota((1, WY), 1)
    column = strip_column(lane)
    weight = (
        jnp.where(lane < 32, x_low, 1.0)
        * jnp.where(lane >= 96, x_high, 1.0)
        * jnp.where(column < 0, y_low, 1.0)
        * jnp.where(column >= WY, y_high, 1.0)
    )
    p, q, s = Planes(p_ref), Planes(q_ref), Planes(s_ref)
    u, v = [Planes(u_ref, c) for c in range(3)], [Planes(v_ref, c) for c in range(3)]
    for planes, first in [(p, 2), (q, 2), (s, 1)] + [(planes, 1) for planes in u + v]:
        planes.clear(first, first + 7)

    def put(planes, i, value, rim):
        planes.put(i + rim, value)
        if i < rim:
            planes.put(i + rim + 8, pltpu.roll(value, 96, 1))
        if i >= 8 - rim:
            planes.put(i + rim - 8, pltpu.roll(value, 32, 1))

    edges = jnp.concatenate([from_left[...], from_right[...]], axis=1)
    for z_half in range(2):
        found = [
            part[z_half] + dot(edges, edge_taps[2 * frame + z_half])
            for frame, part in enumerate((part_own, part_nxt))
        ]
        total, change = (found[0] + found[1]) * 0.25, found[1] - found[0]
        for i in range(16):
            p.put_z(2, 16 * z_half + i, total[8 * i : 8 * i + 8])
            q.put_z(2, 16 * z_half + i, change[8 * i : 8 * i + 8])
    for i in range(8):
        put(p, i, smooth_z(p, i + 2), 2)
        put(q, i, smooth_z(q, i + 2), 2)
    for i in range(8):
        put(s, i, smooth_x(p, i + 2) * weight, 1)
        c_ref[i] = smooth_x(q, i + 2) * weight
    for i in range(8):
        terms, change = gradient_terms(s, i + 1, c_ref[i])
        h_ref[3, i] = change
        for c in range(3):
            h_ref[c, i] = terms[c]
            put(u[c], i, -terms[c] * change, 1)
    for i in range(8):
        for c, value in enumerate(jacobi(u, i + 1, [h_ref[c, i] for c in range(4)])):
            put(v[c], i, value * weight, 1)
    for i in range(8):
        for c, value in enumerate(jacobi(v, i + 1, [h_ref[c, i] for c in range(4)])):
            w_ref[c, NZ * i : NZ * i + NZ, :] = value
    own_lane = iota((NZ, WY), 1)
    rim = (own_lane < 5) | (own_lane >= WY - 5)
    for c in range(3):
        rest = w_ref[c]
        placed = jnp.zeros((8 * NZ, 256), F32)
        for _ in range(3):
            term = rest.astype(BF16)
            rest = rest - term.astype(F32)
            placed = placed + dot(term, place[...])
        for i in range(8):
            for half in range(2):
                x = 8 * half + i
                found = placed[NZ * i : NZ * i + NZ, 128 * half : 128 * half + 128]
                done_ref[c, pl.ds(x, NZ, stride=WX), :] = jnp.where(rim, found, inner[c, x])
        pltpu.make_async_copy(done_ref.at[c], out.at[c], sems.at[c]).start()
    for c in range(3):
        pltpu.make_async_copy(done_ref.at[c], out.at[c], sems.at[c]).wait()


def call(kernel, outs, args, scratch, megabytes, flops, out_space=pltpu.VMEM):
    moved = sum(a.size * a.dtype.itemsize for a in (*args, *outs))
    spec = pl.BlockSpec(memory_space=pltpu.VMEM)
    return pl.pallas_call(
        kernel,
        out_shape=outs,
        in_specs=[spec] * len(args),
        out_specs=tuple([pl.BlockSpec(memory_space=out_space)] * len(outs)),
        scratch_shapes=scratch,
        compiler_params=pltpu.CompilerParams(vmem_limit_bytes=megabytes << 20),
        cost_estimate=pl.CostEstimate(flops=flops, bytes_accessed=moved, transcendentals=0),
    )(*args)


def shape(*dims, dtype=F32):
    return jax.ShapeDtypeStruct(dims, dtype)


def on_device(frames, trailing):
    own = frames[0]

    def passed(value, axis, step):
        count = lax.axis_size(axis)
        pairs = [(i, i + step) for i in range(count) if 0 <= i + step < count]
        return lax.ppermute(value, axis, pairs)

    def swapped(value, axis, first):
        pairs = [(i, i + 1) for i in range(first, lax.axis_size(axis) - 1, 2)]
        return lax.ppermute(value, axis, pairs + [(b, a) for a, b in pairs])

    arriving = passed(own, "ta", -1)
    nxt = jnp.where(lax.axis_index("ta") == lax.axis_size("ta") - 1, trailing, arriving)
    even = lax.axis_index("gx") % 2 == 0

    def rims(frame):
        upper, lower = frame[:, WX - EDGE :], frame[:, :EDGE]
        off_chip = swapped(jnp.where(even, lower, upper), "gx", 1)
        pairs = [[i, i + 1] for i in range(0, lax.axis_size("gx"), 2)]
        both = lax.all_gather(jnp.where(even, upper, lower), "gx", axis_index_groups=pairs)
        on_chip = jnp.where(even, both[1], both[0])
        return jnp.where(even, off_chip, on_chip), jnp.where(even, on_chip, off_chip)

    low_own, high_own = rims(own)
    packed, pick, taps, octet_taps, edge_taps, place, smooth, part_own = call(
        front_kernel,
        tuple(
            shape(*dims, dtype=BF16)
            for dims in ((128, 256), (WY, 256), (WY, WY), (4 * WY, WY), (4, 256, WY), (WY, 256))
        )
        + (shape(22, NZ, WY), shape(2, 128, WY)),
        (own, low_own, high_own),
        [planes_of(32)],
        12,
        10**8,
    )
    low, high = rims(nxt)
    message = shape(128, 128, dtype=BF16)
    to_right, to_left = call(pack_kernel, (message, message), (nxt, low, high, packed, pick), [], 8, 10**8)
    from_left = passed(to_right, "gy", 1)
    from_right = passed(to_left, "gy", -1)
    inner, part_nxt = call(
        inner_kernel,
        (shape(3, WX, NZ, WY), shape(2, 128, WY)),
        (nxt, low, high, taps, octet_taps, smooth),
        [
            planes_of(32),
            planes_of(22),
            pltpu.VMEM((20, NZ, WY), F32),
            pltpu.VMEM((4, 20, NZ, WY), F32),
            planes_of_3(20),
            planes_of_3(18),
        ],
        16,
        10**9,
    )
    (flow,) = call(
        strip_kernel,
        (shape(3, NZ * WX, WY),),
        (inner, part_own, part_nxt, edge_taps, place, from_left, from_right),
        [
            planes_of(12),
            planes_of(12),
            planes_of(10),
            pltpu.VMEM((8, NZ, WY), F32),
            pltpu.VMEM((4, 8, NZ, WY), F32),
            planes_of_3(10),
            planes_of_3(10),
            pltpu.VMEM((3, 8 * NZ, WY), F32),
            pltpu.VMEM((3, NZ * WX, WY), F32),
            pltpu.SemaphoreType.DMA((3,)),
        ],
        16,
        10**8,
        pl.ANY,
    )
    return flow.reshape(1, 3, NZ, WX, WY)


def solution(mesh):
    return jax.shard_map(
        on_device,
        mesh=mesh,
        in_specs=(P("ta", None, "gx", "gy"), P(None, "gx", "gy")),
        out_specs=P("ta", None, None, "gx", "gy"),
        check_vma=False,
    )
```

```python
import jax
import jax.numpy as jnp
from jax import lax
from jax.experimental import pallas as pl
from jax.experimental.pallas import tpu as pltpu
from jax.sharding import PartitionSpec as P

NZ = 32
WX = 16
WY = 128
EDGE = 8
PITCH = 40
F32, BF16 = jnp.float32, jnp.bfloat16


def iota(shape, dim):
    return lax.broadcasted_iota(jnp.int32, shape, dim)


def dot(a, b):
    return jnp.dot(a, b, preferred_element_type=F32)


def y_taps(distance):
    d = jnp.abs(distance)
    tap = jnp.where(d == 0, 6.0, jnp.where(d == 1, 4.0, jnp.where(d == 2, 1.0, 0.0)))
    return tap * (1.0 / 4096.0)


def octet_rows(source, z_half):
    return source[16 * z_half : 16 * z_half + 16].astype(F32).reshape(128, WY).astype(BF16)


def strip_column(lane):
    place = lane & 31
    return jnp.where(place < 16, place - 5, place + 101)


def edge_columns(blocks, pick):
    group = (iota((128, 256), 1) & 127) >> 3
    packed = jnp.zeros((128, 256), F32)
    for (octet, frame), block in blocks.items():
        for z_half in range(2):
            found = dot(octet_rows(block, z_half), pick)
            packed = jnp.where(group == (octet * 2 + frame) * 2 + z_half, found, packed)
    return packed.astype(BF16)


def own_octets(block, frame):
    return {(octet, frame): block[:, 8 * octet - 8 : 8 * octet, :] for octet in (1, 2)}


def front_kernel(
    own, low, high, packed, pick, taps, octet_taps, edge_taps, place, smooth, part, p_ref
):
    row, lane = iota((WY, 256), 0), iota((WY, 256), 1)
    column = (lane & 7) + jnp.where(lane < 128, WY - EDGE, 0)
    pick[...] = jnp.where(row == column, 1.0, 0.0).astype(BF16)
    packed[...] = edge_columns(own_octets(own, 0) | {(0, 0): low, (3, 0): high}, pick[...])

    at, to = row & 31, lane & 127
    hit = ((row >> 5) - 1 == (lane >> 7)) & ((to == at - 5) | (to == at + 101))
    place[...] = jnp.where(hit, 1.0, 0.0).astype(BF16)

    row, lane = iota((WY, WY), 0), iota((WY, WY), 1)
    taps[...] = y_taps(lane - row).astype(BF16)
    strip_taps = y_taps(strip_column(lane) - row)
    for octet in range(4):
        octet_taps[WY * octet : WY * octet + WY, :] = jnp.where((lane >> 5) == octet, strip_taps, 0.0).astype(BF16)

    row, lane = iota((256, WY), 0), iota((256, WY), 1)
    column = (row & 7) + jnp.where(row < 128, -EDGE, WY)
    edge = jnp.where(((row & 127) >> 5) == (lane >> 5), y_taps(strip_column(lane) - column), 0.0)
    for group in range(4):
        edge_taps[group] = jnp.where(((row >> 3) & 3) == group, edge, 0.0).astype(BF16)

    p = Planes(p_ref)
    smooth_yz(p, own_blocks(own) | {0: low[...], 3: high[...]}, taps, octet_taps, part)
    for k in range(22):
        smooth[k] = smooth_x(p, k + 5)


def middle_kernel(nxt, own_packed, pick, taps, octet_taps, packed, middle, part, p_ref):
    packed[...] = own_packed[...] + edge_columns(own_octets(nxt, 1), pick[...])
    p = Planes(p_ref)
    smooth_yz(p, own_blocks(nxt), taps, octet_taps, part)
    for x in range(WX):
        middle[x] = p.get(x + 8)


def pack_kernel(low, high, packed, pick, to_right, to_left):
    both = packed[...] + edge_columns({(0, 1): low, (3, 1): high}, pick[...])
    to_right[...] = both[:, :128]
    to_left[...] = both[:, 128:]


class Planes:
    def __init__(self, ref, index=None):
        self.ref, self.index = ref, index

    def rows(self, start, count, stride=None):
        rows = pl.ds(start, count) if stride is None else pl.ds(start, count, stride=stride)
        return (rows, slice(None)) if self.index is None else (self.index, rows, slice(None))

    def get(self, plane, shift=0):
        return self.ref[self.rows(8 + PITCH * plane + shift, NZ)]

    def put(self, plane, value):
        self.ref[self.rows(8 + PITCH * plane, NZ)] = value

    def put_z(self, plane, z, values):
        self.ref[self.rows(8 + PITCH * plane + z, values.shape[0], PITCH)] = values

    def clear(self, first, last):
        for plane in range(first, last + 2):
            self.ref[self.rows(PITCH * plane, 8)] = jnp.zeros((8, WY), F32)


class Rows:
    def __init__(self, planes, middle):
        self.planes, self.middle = planes, middle

    def get(self, plane):
        return self.middle[plane - 8] if 8 <= plane < 24 else self.planes.get(plane)


def planes_of(count):
    return pltpu.VMEM((8 + PITCH * count, WY), F32)


def planes_of_3(count):
    return pltpu.VMEM((3, 8 + PITCH * count, WY), F32)


def smooth_z(planes, k):
    near = planes.get(k, 1) + planes.get(k, -1)
    far = planes.get(k, 2) + planes.get(k, -2)
    return 6.0 * planes.get(k) + 4.0 * near + far


def smooth_x(planes, k):
    near = planes.get(k + 1) + planes.get(k - 1)
    far = planes.get(k + 2) + planes.get(k - 2)
    return 6.0 * planes.get(k) + 4.0 * near + far


def y_pair(v):
    return pltpu.roll(v, WY - 1, 1), pltpu.roll(v, 1, 1)


def gradient_terms(s, k, change):
    y_next, y_prev = y_pair(s.get(k))
    grads = (s.get(k + 1) - s.get(k - 1), y_next - y_prev, s.get(k, 1) - s.get(k, -1))
    denom = 0.01 + grads[0] * grads[0] + grads[1] * grads[1] + grads[2] * grads[2]
    scale = lax.rsqrt(denom)
    scale = scale * (1.5 - 0.5 * denom * scale * scale)
    return [grad * scale for grad in grads], change * scale


def jacobi(velocity, k, terms):
    means = []
    for planes in velocity:
        y_next, y_prev = y_pair(planes.get(k))
        total = (planes.get(k + 1) + planes.get(k - 1)) + (y_next + y_prev)
        total = total + (planes.get(k, 1) + planes.get(k, -1))
        means.append(total * (1.0 / 6.0))
    common = terms[3] + terms[0] * means[0] + terms[1] * means[1] + terms[2] * means[2]
    return [mean - term * common for mean, term in zip(means, terms)]


def smooth_yz(p, blocks, taps, octet_taps, part, more=None):
    planes = [8 * octet + i for octet in blocks for i in range(8) if 3 <= 8 * octet + i < 29]
    for k in planes:
        p.clear(k, k)
    for z_half in range(2):
        given = None if more is None else more[z_half]
        for octet, block in blocks.items():
            rows = octet_rows(block, z_half)
            found = dot(rows, taps[...])
            for i in range(16):
                p.put_z(8 * octet, 16 * z_half + i, found[8 * i : 8 * i + 8])
            gives = dot(rows, octet_taps[WY * octet : WY * octet + WY, :])
            given = gives if given is None else given + gives
        part[z_half] = given
    for k in planes:
        p.put(k, smooth_z(p, k))


def own_blocks(frame):
    return {octet: frame[:, 8 * octet - 8 : 8 * octet, :] for octet in (1, 2)}


def inside():
    faces = []
    for axis in ("gx", "gy"):
        at = lax.axis_index(axis)
        faces += [jnp.where(at == 0, 0.0, 1.0), jnp.where(at == lax.axis_size(axis) - 1, 0.0, 1.0)]
    return faces


def inner_kernel(
    low, high, taps, octet_taps, smooth, middle, more, inner, part, p_ref, s_ref, c_ref, h_ref, u_ref, v_ref
):
    x_low, x_high, _, _ = inside()

    def weight(x):
        return x_low if x < 0 else x_high if x >= WX else None

    def weighed(value, x):
        return value if weight(x) is None else value * weight(x)

    p, s = Planes(p_ref), Planes(s_ref)
    u, v = [Planes(u_ref, c) for c in range(3)], [Planes(v_ref, c) for c in range(3)]
    s.clear(1, 20)
    for c in range(3):
        u[c].clear(1, 18)
        v[c].clear(1, 16)
    smooth_yz(p, {0: low[...], 3: high[...]}, taps, octet_taps, part, more)
    rows = Rows(p, middle)

    for k in range(22):
        first, second = smooth[k], smooth_x(rows, k + 5)
        s.put(k, weighed((first + second) * 0.25, k - 3))
        if 1 <= k <= 20:
            c_ref[k - 1] = weighed(second - first, k - 3)

    for k in range(20):
        terms, change = gradient_terms(s, k + 1, c_ref[k])
        h_ref[3, k] = change
        for c in range(3):
            h_ref[c, k] = terms[c]
            u[c].put(k, -terms[c] * change)

    for k in range(18):
        for c, value in enumerate(jacobi(u, k + 1, [h_ref[c, k + 1] for c in range(4)])):
            v[c].put(k, weighed(value, k - 1))
    for x in range(WX):
        for c, value in enumerate(jacobi(v, x + 1, [h_ref[c, x + 2] for c in range(4)])):
            inner[c, x] = value


def strip_kernel(
    inner, part_own, part_nxt, edge_taps, place, from_left, from_right, out,
    p_ref, q_ref, s_ref, c_ref, h_ref, u_ref, v_ref, w_ref, done_ref, sems,
):
    x_low, x_high, y_low, y_high = inside()
    lane = iota((1, WY), 1)
    column = strip_column(lane)
    weight = (
        jnp.where(lane < 32, x_low, 1.0)
        * jnp.where(lane >= 96, x_high, 1.0)
        * jnp.where(column < 0, y_low, 1.0)
        * jnp.where(column >= WY, y_high, 1.0)
    )
    p, q, s = Planes(p_ref), Planes(q_ref), Planes(s_ref)
    u, v = [Planes(u_ref, c) for c in range(3)], [Planes(v_ref, c) for c in range(3)]
    for planes, first in [(p, 2), (q, 2), (s, 1)] + [(planes, 1) for planes in u + v]:
        planes.clear(first, first + 7)

    def put(planes, i, value, rim):
        planes.put(i + rim, value)
        if i < rim:
            planes.put(i + rim + 8, pltpu.roll(value, 96, 1))
        if i >= 8 - rim:
            planes.put(i + rim - 8, pltpu.roll(value, 32, 1))

    edges = jnp.concatenate([from_left[...], from_right[...]], axis=1)
    for z_half in range(2):
        found = [
            part[z_half] + dot(edges, edge_taps[2 * frame + z_half])
            for frame, part in enumerate((part_own, part_nxt))
        ]
        total, change = (found[0] + found[1]) * 0.25, found[1] - found[0]
        for i in range(16):
            p.put_z(2, 16 * z_half + i, total[8 * i : 8 * i + 8])
            q.put_z(2, 16 * z_half + i, change[8 * i : 8 * i + 8])
    for i in range(8):
        put(p, i, smooth_z(p, i + 2), 2)
        put(q, i, smooth_z(q, i + 2), 2)
    for i in range(8):
        put(s, i, smooth_x(p, i + 2) * weight, 1)
        c_ref[i] = smooth_x(q, i + 2) * weight
    for i in range(8):
        terms, change = gradient_terms(s, i + 1, c_ref[i])
        h_ref[3, i] = change
        for c in range(3):
            h_ref[c, i] = terms[c]
            put(u[c], i, -terms[c] * change, 1)
    for i in range(8):
        for c, value in enumerate(jacobi(u, i + 1, [h_ref[c, i] for c in range(4)])):
            put(v[c], i, value * weight, 1)
    for i in range(8):
        for c, value in enumerate(jacobi(v, i + 1, [h_ref[c, i] for c in range(4)])):
            w_ref[c, NZ * i : NZ * i + NZ, :] = value
    own_lane = iota((NZ, WY), 1)
    rim = (own_lane < 5) | (own_lane >= WY - 5)
    for c in range(3):
        rest = w_ref[c]
        placed = jnp.zeros((8 * NZ, 256), F32)
        for _ in range(3):
            term = rest.astype(BF16)
            rest = rest - term.astype(F32)
            placed = placed + dot(term, place[...])
        for i in range(8):
            for half in range(2):
                x = 8 * half + i
                found = placed[NZ * i : NZ * i + NZ, 128 * half : 128 * half + 128]
                done_ref[c, pl.ds(x, NZ, stride=WX), :] = jnp.where(rim, found, inner[c, x])
        pltpu.make_async_copy(done_ref.at[c], out.at[c], sems.at[c]).start()
    for c in range(3):
        pltpu.make_async_copy(done_ref.at[c], out.at[c], sems.at[c]).wait()


def call(kernel, outs, args, scratch, megabytes, flops, out_space=pltpu.VMEM):
    moved = sum(a.size * a.dtype.itemsize for a in (*args, *outs))
    spec = pl.BlockSpec(memory_space=pltpu.VMEM)
    return pl.pallas_call(
        kernel,
        out_shape=outs,
        in_specs=[spec] * len(args),
        out_specs=tuple([pl.BlockSpec(memory_space=out_space)] * len(outs)),
        scratch_shapes=scratch,
        compiler_params=pltpu.CompilerParams(vmem_limit_bytes=megabytes << 20),
        cost_estimate=pl.CostEstimate(flops=flops, bytes_accessed=moved, transcendentals=0),
    )(*args)


def shape(*dims, dtype=F32):
    return jax.ShapeDtypeStruct(dims, dtype)


def on_device(frames, trailing):
    own = frames[0]

    def passed(value, axis, step):
        count = lax.axis_size(axis)
        pairs = [(i, i + step) for i in range(count) if 0 <= i + step < count]
        return lax.ppermute(value, axis, pairs)

    def swapped(value, axis, first):
        pairs = [(i, i + 1) for i in range(first, lax.axis_size(axis) - 1, 2)]
        return lax.ppermute(value, axis, pairs + [(b, a) for a, b in pairs])

    arriving = passed(own, "ta", -1)
    nxt = jnp.where(lax.axis_index("ta") == lax.axis_size("ta") - 1, trailing, arriving)
    even = lax.axis_index("gx") % 2 == 0

    def rims(frame):
        upper, lower = frame[:, WX - EDGE :], frame[:, :EDGE]
        off_chip = swapped(jnp.where(even, lower, upper), "gx", 1)
        pairs = [[i, i + 1] for i in range(0, lax.axis_size("gx"), 2)]
        both = lax.all_gather(jnp.where(even, upper, lower), "gx", axis_index_groups=pairs)
        on_chip = jnp.where(even, both[1], both[0])
        return jnp.where(even, off_chip, on_chip), jnp.where(even, on_chip, off_chip)

    low_own, high_own = rims(own)
    packed, pick, taps, octet_taps, edge_taps, place, smooth, part_own = call(
        front_kernel,
        tuple(
            shape(*dims, dtype=BF16)
            for dims in ((128, 256), (WY, 256), (WY, WY), (4 * WY, WY), (4, 256, WY), (WY, 256))
        )
        + (shape(22, NZ, WY), shape(2, 128, WY)),
        (own, low_own, high_own),
        [planes_of(32)],
        12,
        10**8,
    )
    low, high = rims(nxt)
    packed, middle, more = call(
        middle_kernel,
        (shape(128, 256, dtype=BF16), shape(WX, NZ, WY), shape(2, 128, WY)),
        (nxt, packed, pick, taps, octet_taps),
        [planes_of(32)],
        8,
        10**8,
    )
    message = shape(128, 128, dtype=BF16)
    to_right, to_left = call(pack_kernel, (message, message), (low, high, packed, pick), [], 8, 10**8)
    from_left = passed(to_right, "gy", 1)
    from_right = passed(to_left, "gy", -1)
    inner, part_nxt = call(
        inner_kernel,
        (shape(3, WX, NZ, WY), shape(2, 128, WY)),
        (low, high, taps, octet_taps, smooth, middle, more),
        [
            planes_of(32),
            planes_of(22),
            pltpu.VMEM((20, NZ, WY), F32),
            pltpu.VMEM((4, 20, NZ, WY), F32),
            planes_of_3(20),
            planes_of_3(18),
        ],
        16,
        10**9,
    )
    (flow,) = call(
        strip_kernel,
        (shape(3, NZ * WX, WY),),
        (inner, part_own, part_nxt, edge_taps, place, from_left, from_right),
        [
            planes_of(12),
            planes_of(12),
            planes_of(10),
            pltpu.VMEM((8, NZ, WY), F32),
            pltpu.VMEM((4, 8, NZ, WY), F32),
            planes_of_3(10),
            planes_of_3(10),
            pltpu.VMEM((3, 8 * NZ, WY), F32),
            pltpu.VMEM((3, NZ * WX, WY), F32),
            pltpu.SemaphoreType.DMA((3,)),
        ],
        16,
        10**8,
        pl.ANY,
    )
    return flow.reshape(1, 3, NZ, WX, WY)


def solution(mesh):
    return jax.shard_map(
        on_device,
        mesh=mesh,
        in_specs=(P("ta", None, "gx", "gy"), P(None, "gx", "gy")),
        out_specs=P("ta", None, None, "gx", "gy"),
        check_vma=False,
    )
```

```python
import jax
import jax.numpy as jnp
from jax import lax
from jax.experimental import pallas as pl
from jax.experimental.pallas import tpu as pltpu
from jax.sharding import PartitionSpec as P

NZ = 32
WX = 16
WY = 128
EDGE = 8
PITCH = 40
F32, BF16 = jnp.float32, jnp.bfloat16


def iota(shape, dim):
    return lax.broadcasted_iota(jnp.int32, shape, dim)


def dot(a, b):
    return jnp.dot(a, b, preferred_element_type=F32)


def y_taps(distance):
    d = jnp.abs(distance)
    tap = jnp.where(d == 0, 6.0, jnp.where(d == 1, 4.0, jnp.where(d == 2, 1.0, 0.0)))
    return tap * (1.0 / 4096.0)


def octet_rows(source, z_half):
    return source[16 * z_half : 16 * z_half + 16].astype(F32).reshape(128, WY).astype(BF16)


def strip_column(lane):
    place = lane & 31
    return jnp.where(place < 16, place - 5, place + 101)


def edge_columns(blocks, pick):
    group = (iota((128, 256), 1) & 127) >> 3
    packed = jnp.zeros((128, 256), F32)
    for (octet, frame), block in blocks.items():
        for z_half in range(2):
            found = dot(octet_rows(block, z_half), pick)
            packed = jnp.where(group == (octet * 2 + frame) * 2 + z_half, found, packed)
    return packed.astype(BF16)


def own_octets(block, frame):
    return {(octet, frame): block[:, 8 * octet - 8 : 8 * octet, :] for octet in (1, 2)}


def front_kernel(
    own, low, high, packed, pick, taps, octet_taps, edge_taps, place, smooth, part, p_ref
):
    row, lane = iota((WY, 256), 0), iota((WY, 256), 1)
    column = (lane & 7) + jnp.where(lane < 128, WY - EDGE, 0)
    pick[...] = jnp.where(row == column, 1.0, 0.0).astype(BF16)
    packed[...] = edge_columns(own_octets(own, 0) | {(0, 0): low, (3, 0): high}, pick[...])

    at, to = row & 31, lane & 127
    hit = ((row >> 5) - 1 == (lane >> 7)) & ((to == at - 5) | (to == at + 101))
    place[...] = jnp.where(hit, 1.0, 0.0).astype(BF16)

    row, lane = iota((WY, WY), 0), iota((WY, WY), 1)
    taps[...] = y_taps(lane - row).astype(BF16)
    strip_taps = y_taps(strip_column(lane) - row)
    for octet in range(4):
        octet_taps[WY * octet : WY * octet + WY, :] = jnp.where((lane >> 5) == octet, strip_taps, 0.0).astype(BF16)

    row, lane = iota((256, WY), 0), iota((256, WY), 1)
    column = (row & 7) + jnp.where(row < 128, -EDGE, WY)
    edge = jnp.where(((row & 127) >> 5) == (lane >> 5), y_taps(strip_column(lane) - column), 0.0)
    for group in range(4):
        edge_taps[group] = jnp.where(((row >> 3) & 3) == group, edge, 0.0).astype(BF16)

    p = Planes(p_ref)
    smooth_yz(p, own_blocks(own) | {0: low[...], 3: high[...]}, taps, octet_taps, part)
    for k in range(22):
        smooth[k] = smooth_x(p, k + 5)


def middle_kernel(nxt, own_packed, pick, taps, octet_taps, packed, middle, part, p_ref):
    packed[...] = own_packed[...] + edge_columns(own_octets(nxt, 1), pick[...])
    p = Planes(p_ref)
    smooth_yz(p, own_blocks(nxt), taps, octet_taps, part)
    for x in range(WX):
        middle[x] = p.get(x + 8)


def pack_kernel(low, high, packed, pick, to_right, to_left):
    both = packed[...] + edge_columns({(0, 1): low, (3, 1): high}, pick[...])
    to_right[...] = both[:, :128]
    to_left[...] = both[:, 128:]


class Planes:
    def __init__(self, ref, index=None):
        self.ref, self.index = ref, index

    def rows(self, start, count, stride=None):
        rows = pl.ds(start, count) if stride is None else pl.ds(start, count, stride=stride)
        return (rows, slice(None)) if self.index is None else (self.index, rows, slice(None))

    def get(self, plane, shift=0):
        return self.ref[self.rows(8 + PITCH * plane + shift, NZ)]

    def put(self, plane, value):
        self.ref[self.rows(8 + PITCH * plane, NZ)] = value

    def put_z(self, plane, z, values):
        self.ref[self.rows(8 + PITCH * plane + z, values.shape[0], PITCH)] = values

    def clear(self, first, last):
        for plane in range(first, last + 2):
            self.ref[self.rows(PITCH * plane, 8)] = jnp.zeros((8, WY), F32)


class Rows:
    def __init__(self, planes, middle):
        self.planes, self.middle = planes, middle

    def get(self, plane):
        return self.middle[plane - 8] if 8 <= plane < 24 else self.planes.get(plane)


def planes_of(count):
    return pltpu.VMEM((8 + PITCH * count, WY), F32)


def planes_of_3(count):
    return pltpu.VMEM((3, 8 + PITCH * count, WY), F32)


def smooth_z(planes, k):
    near = planes.get(k, 1) + planes.get(k, -1)
    far = planes.get(k, 2) + planes.get(k, -2)
    return 6.0 * planes.get(k) + 4.0 * near + far


def smooth_x(planes, k):
    near = planes.get(k + 1) + planes.get(k - 1)
    far = planes.get(k + 2) + planes.get(k - 2)
    return 6.0 * planes.get(k) + 4.0 * near + far


def y_pair(v):
    return pltpu.roll(v, WY - 1, 1), pltpu.roll(v, 1, 1)


def gradient_terms(s, k, change):
    y_next, y_prev = y_pair(s.get(k))
    grads = (s.get(k + 1) - s.get(k - 1), y_next - y_prev, s.get(k, 1) - s.get(k, -1))
    denom = 0.01 + grads[0] * grads[0] + grads[1] * grads[1] + grads[2] * grads[2]
    scale = lax.rsqrt(denom)
    scale = scale * (1.5 - 0.5 * denom * scale * scale)
    return [grad * scale for grad in grads], change * scale


def jacobi(velocity, k, terms):
    means = []
    for planes in velocity:
        y_next, y_prev = y_pair(planes.get(k))
        total = (planes.get(k + 1) + planes.get(k - 1)) + (y_next + y_prev)
        total = total + (planes.get(k, 1) + planes.get(k, -1))
        means.append(total)
    common = terms[3] + terms[0] * means[0] + terms[1] * means[1] + terms[2] * means[2]
    return [mean - term * common for mean, term in zip(means, terms)]


def smooth_yz(p, blocks, taps, octet_taps, part, more=None):
    planes = [8 * octet + i for octet in blocks for i in range(8) if 3 <= 8 * octet + i < 29]
    for k in planes:
        p.clear(k, k)
    for z_half in range(2):
        given = None if more is None else more[z_half]
        for octet, block in blocks.items():
            rows = octet_rows(block, z_half)
            found = dot(rows, taps[...])
            for i in range(16):
                p.put_z(8 * octet, 16 * z_half + i, found[8 * i : 8 * i + 8])
            gives = dot(rows, octet_taps[WY * octet : WY * octet + WY, :])
            given = gives if given is None else given + gives
        part[z_half] = given
    for k in planes:
        p.put(k, smooth_z(p, k))


def own_blocks(frame):
    return {octet: frame[:, 8 * octet - 8 : 8 * octet, :] for octet in (1, 2)}


def inside():
    faces = []
    for axis in ("gx", "gy"):
        at = lax.axis_index(axis)
        faces += [jnp.where(at == 0, 0.0, 1.0), jnp.where(at == lax.axis_size(axis) - 1, 0.0, 1.0)]
    return faces


def inner_kernel(
    low, high, taps, octet_taps, smooth, middle, more, inner, part, p_ref, s_ref, c_ref, h_ref, u_ref, v_ref
):
    x_low, x_high, _, _ = inside()

    def weight(x):
        return x_low if x < 0 else x_high if x >= WX else None

    def weighed(value, x):
        return value if weight(x) is None else value * weight(x)

    p, s = Planes(p_ref), Planes(s_ref)
    u, v = [Planes(u_ref, c) for c in range(3)], [Planes(v_ref, c) for c in range(3)]
    s.clear(1, 20)
    for c in range(3):
        u[c].clear(1, 18)
        v[c].clear(1, 16)
    smooth_yz(p, {0: low[...], 3: high[...]}, taps, octet_taps, part, more)
    rows = Rows(p, middle)

    for k in range(22):
        first, second = smooth[k], smooth_x(rows, k + 5)
        s.put(k, weighed((first + second) * 0.25, k - 3))
        if 1 <= k <= 20:
            c_ref[k - 1] = weighed(second - first, k - 3)

    for k in range(20):
        terms, change = gradient_terms(s, k + 1, c_ref[k])
        h_ref[3, k] = 6.0 * change
        for c in range(3):
            h_ref[c, k] = terms[c]
            u[c].put(k, -terms[c] * change)

    for k in range(18):
        for c, value in enumerate(jacobi(u, k + 1, [h_ref[c, k + 1] for c in range(4)])):
            v[c].put(k, weighed(value, k - 1))
    for x in range(WX):
        for c, value in enumerate(jacobi(v, x + 1, [h_ref[c, x + 2] for c in range(3)] + [6.0 * h_ref[3, x + 2]])):
            inner[c, x] = value * (1.0 / 36.0)


def strip_kernel(
    inner, part_own, part_nxt, edge_taps, place, from_left, from_right, out,
    p_ref, q_ref, s_ref, c_ref, h_ref, u_ref, v_ref, w_ref, done_ref, sems,
):
    x_low, x_high, y_low, y_high = inside()
    lane = iota((1, WY), 1)
    column = strip_column(lane)
    weight = (
        jnp.where(lane < 32, x_low, 1.0)
        * jnp.where(lane >= 96, x_high, 1.0)
        * jnp.where(column < 0, y_low, 1.0)
        * jnp.where(column >= WY, y_high, 1.0)
    )
    p, q, s = Planes(p_ref), Planes(q_ref), Planes(s_ref)
    u, v = [Planes(u_ref, c) for c in range(3)], [Planes(v_ref, c) for c in range(3)]
    for planes, first in [(p, 2), (q, 2), (s, 1)] + [(planes, 1) for planes in u + v]:
        planes.clear(first, first + 7)

    def put(planes, i, value, rim):
        planes.put(i + rim, value)
        if i < rim:
            planes.put(i + rim + 8, pltpu.roll(value, 96, 1))
        if i >= 8 - rim:
            planes.put(i + rim - 8, pltpu.roll(value, 32, 1))

    edges = jnp.concatenate([from_left[...], from_right[...]], axis=1)
    for z_half in range(2):
        found = [
            part[z_half] + dot(edges, edge_taps[2 * frame + z_half])
            for frame, part in enumerate((part_own, part_nxt))
        ]
        total, change = (found[0] + found[1]) * 0.25, found[1] - found[0]
        for i in range(16):
            p.put_z(2, 16 * z_half + i, total[8 * i : 8 * i + 8])
            q.put_z(2, 16 * z_half + i, change[8 * i : 8 * i + 8])
    for i in range(8):
        put(p, i, smooth_z(p, i + 2), 2)
        put(q, i, smooth_z(q, i + 2), 2)
    for i in range(8):
        put(s, i, smooth_x(p, i + 2) * weight, 1)
        c_ref[i] = smooth_x(q, i + 2) * weight
    for i in range(8):
        terms, change = gradient_terms(s, i + 1, c_ref[i])
        h_ref[3, i] = 6.0 * change
        for c in range(3):
            h_ref[c, i] = terms[c]
            put(u[c], i, -terms[c] * change, 1)
    for i in range(8):
        for c, value in enumerate(jacobi(u, i + 1, [h_ref[c, i] for c in range(4)])):
            put(v[c], i, value * weight, 1)
    for i in range(8):
        for c, value in enumerate(jacobi(v, i + 1, [h_ref[c, i] for c in range(3)] + [6.0 * h_ref[3, i]])):
            w_ref[c, NZ * i : NZ * i + NZ, :] = value * (1.0 / 36.0)
    own_lane = iota((NZ, WY), 1)
    rim = (own_lane < 5) | (own_lane >= WY - 5)
    for c in range(3):
        rest = w_ref[c]
        placed = jnp.zeros((8 * NZ, 256), F32)
        for _ in range(3):
            term = rest.astype(BF16)
            rest = rest - term.astype(F32)
            placed = placed + dot(term, place[...])
        for i in range(8):
            for half in range(2):
                x = 8 * half + i
                found = placed[NZ * i : NZ * i + NZ, 128 * half : 128 * half + 128]
                done_ref[c, pl.ds(x, NZ, stride=WX), :] = jnp.where(rim, found, inner[c, x])
        pltpu.make_async_copy(done_ref.at[c], out.at[c], sems.at[c]).start()
    for c in range(3):
        pltpu.make_async_copy(done_ref.at[c], out.at[c], sems.at[c]).wait()


def call(kernel, outs, args, scratch, megabytes, flops, out_space=pltpu.VMEM):
    moved = sum(a.size * a.dtype.itemsize for a in (*args, *outs))
    spec = pl.BlockSpec(memory_space=pltpu.VMEM)
    return pl.pallas_call(
        kernel,
        out_shape=outs,
        in_specs=[spec] * len(args),
        out_specs=tuple([pl.BlockSpec(memory_space=out_space)] * len(outs)),
        scratch_shapes=scratch,
        compiler_params=pltpu.CompilerParams(vmem_limit_bytes=megabytes << 20),
        cost_estimate=pl.CostEstimate(flops=flops, bytes_accessed=moved, transcendentals=0),
    )(*args)


def shape(*dims, dtype=F32):
    return jax.ShapeDtypeStruct(dims, dtype)


def on_device(frames, trailing):
    own = frames[0]

    def passed(value, axis, step):
        count = lax.axis_size(axis)
        pairs = [(i, i + step) for i in range(count) if 0 <= i + step < count]
        return lax.ppermute(value, axis, pairs)

    def swapped(value, axis, first):
        pairs = [(i, i + 1) for i in range(first, lax.axis_size(axis) - 1, 2)]
        return lax.ppermute(value, axis, pairs + [(b, a) for a, b in pairs])

    arriving = passed(own, "ta", -1)
    nxt = jnp.where(lax.axis_index("ta") == lax.axis_size("ta") - 1, trailing, arriving)
    even = lax.axis_index("gx") % 2 == 0

    def rims(frame):
        upper, lower = frame[:, WX - EDGE :], frame[:, :EDGE]
        off_chip = swapped(jnp.where(even, lower, upper), "gx", 1)
        pairs = [[i, i + 1] for i in range(0, lax.axis_size("gx"), 2)]
        both = lax.all_gather(jnp.where(even, upper, lower), "gx", axis_index_groups=pairs)
        on_chip = jnp.where(even, both[1], both[0])
        return jnp.where(even, off_chip, on_chip), jnp.where(even, on_chip, off_chip)

    low_own, high_own = rims(own)
    packed, pick, taps, octet_taps, edge_taps, place, smooth, part_own = call(
        front_kernel,
        tuple(
            shape(*dims, dtype=BF16)
            for dims in ((128, 256), (WY, 256), (WY, WY), (4 * WY, WY), (4, 256, WY), (WY, 256))
        )
        + (shape(22, NZ, WY), shape(2, 128, WY)),
        (own, low_own, high_own),
        [planes_of(32)],
        12,
        10**8,
    )
    low, high = rims(nxt)
    packed, middle, more = call(
        middle_kernel,
        (shape(128, 256, dtype=BF16), shape(WX, NZ, WY), shape(2, 128, WY)),
        (nxt, packed, pick, taps, octet_taps),
        [planes_of(32)],
        8,
        10**8,
    )
    message = shape(128, 128, dtype=BF16)
    to_right, to_left = call(pack_kernel, (message, message), (low, high, packed, pick), [], 8, 10**8)
    from_left = passed(to_right, "gy", 1)
    from_right = passed(to_left, "gy", -1)
    inner, part_nxt = call(
        inner_kernel,
        (shape(3, WX, NZ, WY), shape(2, 128, WY)),
        (low, high, taps, octet_taps, smooth, middle, more),
        [
            planes_of(32),
            planes_of(22),
            pltpu.VMEM((20, NZ, WY), F32),
            pltpu.VMEM((4, 20, NZ, WY), F32),
            planes_of_3(20),
            planes_of_3(18),
        ],
        16,
        10**9,
    )
    (flow,) = call(
        strip_kernel,
        (shape(3, NZ * WX, WY),),
        (inner, part_own, part_nxt, edge_taps, place, from_left, from_right),
        [
            planes_of(12),
            planes_of(12),
            planes_of(10),
            pltpu.VMEM((8, NZ, WY), F32),
            pltpu.VMEM((4, 8, NZ, WY), F32),
            planes_of_3(10),
            planes_of_3(10),
            pltpu.VMEM((3, 8 * NZ, WY), F32),
            pltpu.VMEM((3, NZ * WX, WY), F32),
            pltpu.SemaphoreType.DMA((3,)),
        ],
        16,
        10**8,
        pl.ANY,
    )
    return flow.reshape(1, 3, NZ, WX, WY)


def solution(mesh):
    return jax.shard_map(
        on_device,
        mesh=mesh,
        in_specs=(P("ta", None, "gx", "gy"), P(None, "gx", "gy")),
        out_specs=P("ta", None, None, "gx", "gy"),
        check_vma=False,
    )
```
